32 devices in a mesh: grp: 2 (over core), row: 2 (over y), col: 8 (over z, x).
Axes of the slice: x: 2, y: 2, z: 4, core: 2. Of those that a mesh axis runs over, the one named last changes fastest.
Arguments:
- load: float32 [4, 8, 1024, 256], P(('grp', 'row'), 'col'), may hold values from -6 to 6
- guess: float32 [4, 8, 1024, 256], P(('grp', 'row'), 'col'), may hold values from -6 to 6
- interface_op: bfloat16 [4, 8, 1024, 1024], P(('grp', 'row'), 'col'), may hold values from -1 to 5
- precond: bfloat16 [4, 8, 1024, 1024], P(('grp', 'row'), 'col'), may hold values from -1 to 2
- basis: bfloat16 [4, 8, 1024, 64], P(('grp', 'row'), 'col'), may hold values from -0.375 to 0.375
- coarse_inverse: bfloat16 [2048, 2048], P(('grp', 'row'), 'col'), may hold values from -0.1875 to 0.1875
- edge_rows: int32 [4, 8, 1024], P(('grp', 'row'), 'col'), may hold values from 0 to 1023, each once within a row
- coarse_slot: int32 [4, 8, 64], P(('grp', 'row'), 'col'), may hold values from 0 to 63, each once within a row
Outputs:
- displacement: float32 [4, 8, 1024, 256], P(('grp', 'row'), 'col')
The draws below stay inside these ranges and needn't reach their ends.
Inputs may be any that keep to these rules, and one draw needn't show every extreme that they name: `edge_rows`: each subdomain lists each of its 1024 interface rows once. `coarse_slot`: each subdomain gives each of its 64 basis vectors a different offset.
All inputs are finite; a program needn't handle non-finite values.
Results may differ from the reference program's by a relative error of at most 0.0095.
Values may be sent and summed in bfloat16 or wider, within the bound.
No kernel may reach another device: no remote copies, remote signals or barrier semaphores. Data moves between devices by JAX's collectives and lax.ppermute only.
A program may use at most 64 MiB of HBM per device.

```python
import math
import jax
import jax.numpy as jnp
from jax import lax

NI = 1024
NB = 64
R = 256
ITERS = 2
GRID_R = 4
GRID_C = 8
COARSE = 2048


def dominant_matrix(key, off_scale, diag_lo, diag_hi):
    first, second = jax.random.split(key)
    shape = (GRID_R, GRID_C, NI, NI)
    coupling = jax.random.truncated_normal(first, -4.0, 4.0, shape, jnp.float32)
    diagonal = jax.random.uniform(second, (GRID_R, GRID_C, NI), jnp.float32, diag_lo, diag_hi)
    matrix = coupling * (off_scale / math.sqrt(NI)) + diagonal[..., None] * jnp.eye(NI, dtype=jnp.float32)
    return matrix.astype(jnp.bfloat16)


def draw_interface_op(key, part):
    return dominant_matrix(jax.random.fold_in(key, 11), 0.6, 1.0, 3.0)


def draw_precond(key, part):
    return dominant_matrix(jax.random.fold_in(key, 23), 0.15, 0.3, 0.9)


def with_spikes(values, rng, source, target, shards_of, factor):
    owner, partner = [(jnp.arange(values.shape[axis_at]) // (values.shape[axis_at] // shards_of)).reshape([-1 if axis == axis_at else 1 for axis in range(values.ndim)]) for axis_at in (source, target)]
    chosen = jax.random.permutation(rng, shards_of)[partner]
    strong = (owner == chosen) | (owner == (partner + shards_of // 2) % shards_of)
    return jnp.where(strong, factor * values, values)


def steps_of(stream_key, dims, cuts, low, top_value):
    def one(axis_at, shards_of):
        draws = jax.random.uniform(jax.random.fold_in(jax.random.fold_in(stream_key, 6), axis_at), (shards_of,), jnp.float32, low / len(cuts), top_value / len(cuts))
        return jnp.repeat(jnp.exp(draws), dims[axis_at] // shards_of).reshape((-1,) + (1,) * (len(dims) - axis_at - 1))

    gain = one(*cuts[0])
    for cut in cuts[1:]:
        gain = gain * one(*cut)
    return gain


def bell_draw(own_key, dims, spread, most, shards=(), kind=jnp.bfloat16):
    level = steps_of(own_key, dims, shards, -0.22, 0.18) if shards else 1.0
    array = jax.random.normal(own_key, dims, jnp.float32) * spread * level
    return jnp.minimum(jnp.maximum(array, -most), most).astype(kind)


def gaussian_with(key, extent, width, reach, cuts, heavy, kind=jnp.bfloat16):
    array = width * jax.random.normal(key, extent, jnp.float32)
    if cuts:
        array = array * steps_of(key, extent, cuts, -0.22, 0.18)
    return jnp.clip(with_spikes(array, jax.random.fold_in(key, 3), *heavy), -reach, reach).astype(kind)


def setup_inputs(seed: int = 0) -> dict:
    key_of = jax.random.split(jax.random.key(seed), 9)
    return {
        "load": bell_draw(key_of[0], (GRID_R, GRID_C, NI, R), 1.0, 6.0, ((0, 4), (1, 8)), jnp.float32),
        "guess": bell_draw(key_of[1], (GRID_R, GRID_C, NI, R), 1.0, 6.0, ((0, 4), (1, 8)), jnp.float32),
        "interface_op": draw_interface_op(jax.random.fold_in(key_of[8], 71), 0),
        "precond": draw_precond(jax.random.fold_in(key_of[8], 71), 0),
        "basis": bell_draw(key_of[4], (GRID_R, GRID_C, NI, NB), (NI // 4) ** -0.5, 0.375, ((0, 4), (1, 8))),
        "coarse_inverse": gaussian_with(key_of[5], (COARSE, COARSE), COARSE ** -0.5, 0.1875, ((0, 4), (1, 8)), (1, 0, 8, 2.0)),
        "edge_rows": jax.vmap(lambda own: jax.random.permutation(own, NI))(jax.random.split(key_of[6], GRID_R * GRID_C)).reshape((GRID_R, GRID_C, NI)).astype(jnp.int32),
        "coarse_slot": jax.vmap(lambda own: jax.random.permutation(own, NB))(jax.random.split(key_of[7], GRID_R * GRID_C)).reshape((GRID_R, GRID_C, NB)).astype(jnp.int32),
    }


OMEGA = 0.6


def local_apply(mats, vecs):
    flat_mats = mats.reshape((GRID_R * GRID_C,) + mats.shape[2:])
    flat_vecs = vecs.reshape((GRID_R * GRID_C,) + vecs.shape[2:])
    result = lax.map(lambda pair: jnp.dot(pair[0], pair[1], preferred_element_type=jnp.float32), (flat_mats, flat_vecs))
    return result.reshape((GRID_R, GRID_C) + result.shape[1:])


def edge_values(field, edge_rows):
    picked = jnp.take_along_axis(field, edge_rows[..., None], axis=2)
    return picked.reshape(GRID_R, GRID_C, 4, NI // 4, R)


def neighbour_values(edges):
    zero_col = jnp.zeros_like(edges[:, :1, 0])
    west = jnp.concatenate([zero_col, edges[:, :-1, 1]], axis=1)
    east = jnp.concatenate([edges[:, 1:, 0], zero_col], axis=1)
    zero_row = jnp.zeros_like(edges[:1, :, 0])
    south = jnp.concatenate([zero_row, edges[:-1, :, 3]], axis=0)
    north = jnp.concatenate([edges[1:, :, 2], zero_row], axis=0)
    return jnp.stack([west, east, south, north], axis=2)


def place(values, inverse):
    flat = values.reshape(GRID_R, GRID_C, NI, R)
    return jnp.take_along_axis(flat, inverse[..., None], axis=2)


def reference(load, guess, interface_op, precond, basis, coarse_inverse, edge_rows, coarse_slot):
    inverse = jnp.argsort(edge_rows, axis=2).astype(jnp.int32)
    slot_inverse = jnp.argsort(coarse_slot, axis=2).astype(jnp.int32)
    grid_row = jnp.arange(GRID_R, dtype=jnp.int32)[:, None] + jnp.zeros((GRID_R, GRID_C), jnp.int32)
    grid_col = jnp.arange(GRID_C, dtype=jnp.int32)[None, :] + jnp.zeros((GRID_R, GRID_C), jnp.int32)
    present = jnp.stack([grid_col > 0, grid_col < GRID_C - 1, grid_row > 0, grid_row < GRID_R - 1], axis=2)
    present = present.astype(jnp.float32)[..., None, None]
    basis_t = jnp.swapaxes(basis, 2, 3)
    current = guess
    for sweep in range(ITERS):
        applied = local_apply(interface_op, current.astype(jnp.bfloat16))
        resid = load - applied - place(neighbour_values(edge_values(applied, edge_rows)), inverse)
        resid_bf = resid.astype(jnp.bfloat16)
        local_fix = local_apply(precond, resid_bf)
        own = edge_values(local_fix, edge_rows)
        smooth_fix = local_fix + 0.5 * place(present * (neighbour_values(own) - own), inverse)
        coarse_res = local_apply(basis_t, resid_bf).astype(jnp.bfloat16)
        coarse_vec = jnp.take_along_axis(coarse_res, slot_inverse[..., None], axis=2).reshape(COARSE, R)
        coarse_sol = jnp.dot(coarse_inverse, coarse_vec, preferred_element_type=jnp.float32).astype(jnp.bfloat16)
        coarse_sol = coarse_sol.reshape(GRID_R, GRID_C, NB, R)
        picked = jnp.take_along_axis(coarse_sol, coarse_slot[..., None], axis=2)
        coarse_fix = local_apply(basis, picked)
        current = current + OMEGA * (smooth_fix + coarse_fix)
    return current
```

```python
import functools

import jax
import jax.numpy as jnp
from jax import lax
from jax.experimental import pallas as pl
from jax.experimental.pallas import tpu as pltpu
from jax.sharding import PartitionSpec as P

ITERS = 2
OMEGA = 0.6
AXES = ("grp", "row", "col")
BF = jnp.bfloat16
F32 = jnp.float32
VMEM_LIMIT = 24 << 20


def dot(a, b):
    return jnp.dot(a, b, preferred_element_type=F32)


def call(kernel, outs, args, flops, scratch=(), name=None):
    moved = sum(a.size * a.dtype.itemsize for a in args)
    return pl.pallas_call(
        kernel,
        out_shape=outs,
        scratch_shapes=list(scratch),
        compiler_params=pltpu.CompilerParams(vmem_limit_bytes=VMEM_LIMIT),
        cost_estimate=pl.CostEstimate(flops=flops, transcendentals=0, bytes_accessed=moved),
        name=name,
    )(*args)


def shape(dims, dtype):
    return jax.ShapeDtypeStruct(tuple(dims), dtype)


def pairs_of(sizes, where):
    grps, rows, cols = sizes
    flat = lambda g, r, c: (g * rows + r) * cols + c
    return [
        (flat(g, r, c), flat(*where(g, r, c)))
        for g in range(grps)
        for r in range(rows)
        for c in range(cols)
    ]


def matching(sizes, odd, along_cols):
    grps, rows, cols = sizes
    count = cols if along_cols else grps * rows

    def where(g, r, c):
        at = c if along_cols else g * rows + r
        to = at + 1 if at % 2 == odd else at - 1
        if 0 <= to < count:
            return (g, r, to) if along_cols else (to // rows, to % rows, c)
        if along_cols and grps == 2:
            return (1 - g, r, c)
        if not along_cols and cols % 4 == 0:
            return (g, r, c ^ 2)
        return (g, r, c)

    return pairs_of(sizes, where)


def send(value, pairs):
    return lax.ppermute(value, AXES, pairs)


def start_kernel(n, order_ref, op_ref, u_ref, sel_ref, applied_ref, *edges):
    order = jnp.broadcast_to(order_ref[...], (128, n)).T
    lanes = lax.broadcasted_iota(jnp.int32, (n, 128), 1)
    for j in range(n // 128):
        sel_ref[:, j * 128 : (j + 1) * 128] = jnp.where(order == lanes + j * 128, 1.0, 0.0).astype(BF)
    apply_kernel(op_ref, u_ref[...], sel_ref, applied_ref, edges)


def apply_kernel(op_ref, u, sel_ref, applied_ref, edges):
    applied = dot(op_ref[...], u.astype(BF))
    applied_ref[...] = applied
    split_edges(applied, sel_ref, edges)


def split_edges(field, sel_ref, edges):
    field = field.astype(BF)
    part = field.shape[0] // 4
    for m, edge in enumerate(edges):
        edge[...] = dot(sel_ref[m * part : (m + 1) * part, :], field).astype(BF)


def tables_kernel(order_ref, basis_t_ref, slot_ref, scatter_ref, based_ref, based_t_ref):
    n = scatter_ref.shape[0]
    part = n // 4
    for m in range(4):
        cols = slice(m * part, (m + 1) * part)
        rows = lax.broadcasted_iota(jnp.int32, (n, part), 0)
        scatter_ref[:, cols] = jnp.where(rows == order_ref[:, cols], 1.0, 0.0).astype(BF)
    nb = basis_t_ref.shape[0]
    pick = lax.broadcasted_iota(jnp.int32, (nb, nb), 0) == slot_ref[...]
    based_t = dot(jnp.where(pick, 1.0, 0.0).astype(BF), basis_t_ref[...])
    based_t_ref[...] = based_t.astype(BF)
    based_ref[...] = based_t.T.astype(BF)


def shared(sizes):
    grps, rows, cols = sizes
    a = lax.axis_index("grp") * rows + lax.axis_index("row")
    c = lax.axis_index("col")

    def partner(at, count, odd):
        up = at % 2 == odd
        return jnp.where(up, at + 1 < count, at > 0)

    return [
        partner(c, cols, 0),
        partner(c, cols, 1),
        partner(a, grps * rows, 0),
        partner(a, grps * rows, 1),
    ]


def resid_kernel(sizes, load_ref, applied_ref, scatter_ref, based_t_ref, n0, n1, n2, n3, resid_ref, coarse_ref, gathered):
    part = n0.shape[0]
    for m, (there, near) in enumerate(zip(shared(sizes), (n0, n1, n2, n3))):
        gathered[m * part : (m + 1) * part, :] = jnp.where(there, near[...], jnp.zeros_like(near))
    resid = load_ref[...] - applied_ref[...] - dot(scatter_ref[...], gathered[...])
    resid = resid.astype(BF)
    resid_ref[...] = resid
    coarse_ref[...] = dot(based_t_ref[...], resid).astype(BF)


def fix_kernel(pre_ref, resid_ref, sel_ref, fix_ref, *edges):
    fix = dot(pre_ref[...], resid_ref[...])
    fix_ref[...] = fix
    split_edges(fix, sel_ref, edges)


def update(sizes, u_ref, fix_ref, scatter_ref, based_ref, own, near, mine_ref, others, gathered):
    part = own[0].shape[0]
    for m, there in enumerate(shared(sizes)):
        jump = near[m][...].astype(F32) - own[m][...].astype(F32)
        gathered[m * part : (m + 1) * part, :] = jnp.where(there, jump, 0.0).astype(BF)
    solved = mine_ref[...]
    for other in others:
        solved = solved + other[...].astype(F32)
    coarse = dot(based_ref[...], solved.astype(BF))
    smooth = fix_ref[...] + 0.5 * dot(scatter_ref[...], gathered[...])
    return u_ref[...] + OMEGA * (smooth + coarse)


def next_kernel(sizes, others, op_ref, sel_ref, u_ref, fix_ref, scatter_ref, based_ref, *refs):
    own, near, mine, rest, refs = refs[:4], refs[4:8], refs[8], refs[9 : 9 + others], refs[9 + others :]
    out_ref, applied_ref, edges, gathered = refs[0], refs[1], refs[2:6], refs[6]
    u = update(sizes, u_ref, fix_ref, scatter_ref, based_ref, own, near, mine, rest, gathered)
    out_ref[...] = u
    apply_kernel(op_ref, u, sel_ref, applied_ref, edges)


def last_kernel(sizes, others, u_ref, fix_ref, scatter_ref, based_ref, *refs):
    own, near, mine, rest, refs = refs[:4], refs[4:8], refs[8], refs[9 : 9 + others], refs[9 + others :]
    out_ref, gathered = refs
    out_ref[...] = update(sizes, u_ref, fix_ref, scatter_ref, based_ref, own, near, mine, rest, gathered)


def regroup_kernel(geometry, nb, inverse_ref, *blocks):
    grid_rows, ratio, lines = geometry
    c = lax.axis_index("col")
    owner = c // ratio
    for k, block in enumerate(blocks):
        target = k ^ owner
        parity, pair = target % 2, target // 2
        for line in range(lines):
            rows = pl.ds(pl.multiple_of((2 * line + parity) * nb, nb), nb)
            cols = pl.ds(pl.multiple_of(pair * 2 * nb, 2 * nb), 2 * nb)
            block[line * nb : (line + 1) * nb, :] = inverse_ref[rows, cols]


def coarse_kernel(geometry, row_size, nb, moves, *refs):
    grid_rows, ratio, lines = geometry
    blocks, refs = refs[:grid_rows], refs[grid_rows:]
    vectors, refs = refs[: len(moves)], refs[len(moves) :]
    mine_ref, others, (stack, total) = refs[0], refs[1:lines], refs[lines:]
    g, r, c = (lax.axis_index(axis) for axis in AXES)
    for (dg, dr, dc), vector in zip(moves, vectors):
        at = (((g ^ dg) * row_size + (r ^ dr)) * 2 + ((c % 2) ^ dc)) * nb
        stack[pl.ds(pl.multiple_of(at, nb), nb), :] = vector[...]
    acc = None
    for k, block in enumerate(blocks):
        owner = k ^ (c % grid_rows)
        part = dot(block[...], stack[pl.ds(pl.multiple_of(owner * 2 * nb, 2 * nb), 2 * nb), :])
        acc = part if acc is None else acc + part
    total[...] = acc
    line = c // 2
    for k in range(lines):
        got = total[pl.ds(pl.multiple_of((line ^ k) * nb, nb), nb), :]
        if k == 0:
            mine_ref[...] = got
        else:
            others[k - 1][...] = got.astype(BF)


def body(load, guess, interface_op, precond, basis, coarse_inverse, edge_rows, coarse_slot):
    sizes = tuple(lax.axis_size(axis) for axis in AXES)
    grps, row_size, cols = sizes
    grid_rows = grps * row_size
    load, u, op, pre = load[0, 0], guess[0, 0], interface_op[0, 0], precond[0, 0]
    basis_t = jnp.swapaxes(basis[0, 0], 0, 1)
    slot = coarse_slot[0]
    n, cases = load.shape
    nb = basis_t.shape[0]
    part = n // 4
    ratio, lines = cols // grid_rows, cols // 2
    geometry = (grid_rows, ratio, lines)

    a = lax.axis_index("grp") * row_size + lax.axis_index("row")
    c = lax.axis_index("col")
    lists = edge_rows[0, 0].reshape(4, part)
    west, east, south, north = (lists[k] for k in range(4))
    even_c, even_a = c % 2 == 0, a % 2 == 0
    order = jnp.concatenate(
        [
            jnp.where(even_c, east, west),
            jnp.where(even_c, west, east),
            jnp.where(even_a, north, south),
            jnp.where(even_a, south, north),
        ]
    ).reshape(1, n)

    halo_pairs = [
        matching(sizes, 0, True),
        matching(sizes, 1, True),
        matching(sizes, 0, False),
        matching(sizes, 1, False),
    ]
    moves = [
        (dg, dr, dc) for dr in range(row_size) for dc in range(2) for dg in range(grps)
    ]

    def swap_pairs(dg, dr, dc):
        return pairs_of(sizes, lambda g, r, c: (g ^ dg, r ^ dr, c ^ dc))

    field = shape((n, cases), F32)
    edge = shape((part, cases), BF)
    square = shape((n, n), BF)
    flops = 2 * n * n * cases

    sel, applied, *edges = call(
        functools.partial(start_kernel, n), [square, field] + [edge] * 4, [order, op, u], 2 * flops, name="start"
    )
    near = [send(e, p) for e, p in zip(edges, halo_pairs)]
    scatter, based, based_t = call(
        tables_kernel,
        [square, shape((n, nb), BF), shape((nb, n), BF)],
        [order, basis_t, slot],
        n * n,
        name="tables",
    )
    blocks = call(
        functools.partial(regroup_kernel, geometry, nb),
        [shape((lines * nb, 2 * nb), BF)] * grid_rows,
        [coarse_inverse],
        n,
        name="regroup",
    )

    def target(k):
        return pairs_of(sizes, lambda g, r, c: (g, r, (c % ratio) * grid_rows + (k ^ (c // ratio))))

    blocks = [send(block, target(k)) for k, block in enumerate(blocks)]

    gathered = [pltpu.VMEM((n, cases), BF)]
    for sweep in range(ITERS):
        resid, coarse = call(
            functools.partial(resid_kernel, sizes),
            [shape((n, cases), BF), shape((nb, cases), BF)],
            [load, applied, scatter, based_t, *near],
            flops,
            gathered,
            name="resid",
        )
        vectors = {}
        for dr in range(row_size):
            for dc in range(2):
                far = coarse if (dr, dc) == (0, 0) else send(coarse, swap_pairs(0, dr, dc))
                vectors[0, dr, dc] = far
        for dr in range(row_size):
            for dc in range(2):
                for dg in range(1, grps):
                    vectors[dg, dr, dc] = send(vectors[0, dr, dc], swap_pairs(dg, 0, 0))
        fix, *own = call(
            fix_kernel, [field] + [edge] * 4, [pre, resid, sel], 2 * flops, name="fix"
        )
        near = [send(e, p) for e, p in zip(own, halo_pairs)]
        mine, *others = call(
            functools.partial(coarse_kernel, geometry, row_size, nb, moves),
            [shape((nb, cases), F32)] + [shape((nb, cases), BF)] * (lines - 1),
            [*blocks, *(vectors[move] for move in moves)],
            2 * lines * nb * 2 * nb * grid_rows * cases,
            [pltpu.VMEM((2 * grid_rows * nb, cases), BF), pltpu.VMEM((lines * nb, cases), F32)],
            name="coarse",
        )
        others = [send(o, swap_pairs(0, 0, 2 * (k + 1))) for k, o in enumerate(others)]
        args = [u, fix, scatter, based, *own, *near, mine, *others]
        if sweep < ITERS - 1:
            u, applied, *edges = call(
                functools.partial(next_kernel, sizes, len(others)),
                [field, field] + [edge] * 4,
                [op, sel, *args],
                3 * flops,
                gathered,
                name="next",
            )
            near = [send(e, p) for e, p in zip(edges, halo_pairs)]
        else:
            u = call(functools.partial(last_kernel, sizes, len(others)), field, args, flops, gathered, name="last")
    return u[None, None]


def solution(mesh):
    cells = P(("grp", "row"), "col", None, None)
    lists = P(("grp", "row"), "col", None)
    return jax.shard_map(
        body,
        mesh=mesh,
        in_specs=(cells, cells, cells, cells, cells, P(("grp", "row"), "col"), lists, lists),
        out_specs=cells,
        check_vma=False,
    )
```

```python
import functools

import jax
import jax.numpy as jnp
from jax import lax
from jax.experimental import pallas as pl
from jax.experimental.pallas import tpu as pltpu
from jax.sharding import PartitionSpec as P


ITERS = 2
OMEGA = 0.6
AXES = ("grp", "row", "col")
BF = jnp.bfloat16
F32 = jnp.float32
VMEM_LIMIT = 24 << 20


def dot(a, b):
    return jnp.dot(a, b, preferred_element_type=F32)


def call(kernel, outs, args, flops, scratch=()):
    moved = sum(a.size * a.dtype.itemsize for a in args)
    return pl.pallas_call(
        kernel,
        out_shape=outs,
        scratch_shapes=list(scratch),
        compiler_params=pltpu.CompilerParams(vmem_limit_bytes=VMEM_LIMIT),
        cost_estimate=pl.CostEstimate(flops=flops, transcendentals=0, bytes_accessed=moved),
    )(*args)


def shape(dims, dtype):
    return jax.ShapeDtypeStruct(tuple(dims), dtype)


def pairs_of(sizes, where):
    grps, rows, cols = sizes
    flat = lambda g, r, c: (g * rows + r) * cols + c
    return [
        (flat(g, r, c), flat(*where(g, r, c)))
        for g in range(grps)
        for r in range(rows)
        for c in range(cols)
    ]


def matching(sizes, odd, along_cols):
    grps, rows, cols = sizes
    count = cols if along_cols else grps * rows

    def where(g, r, c):
        at = c if along_cols else g * rows + r
        to = at + 1 if at % 2 == odd else at - 1
        if 0 <= to < count:
            return (g, r, to) if along_cols else (to // rows, to % rows, c)
        if along_cols and grps == 2:
            return (1 - g, r, c)
        if not along_cols and cols % 4 == 0:
            return (g, r, c ^ 2)
        return (g, r, c)

    return pairs_of(sizes, where)


def send(value, pairs):
    return lax.ppermute(value, AXES, pairs)


def edge_of(sizes, m):
    _, rows, _ = sizes
    if m < 2:
        at, up, down = lax.axis_index("col"), 1, 0
    else:
        at, up, down = lax.axis_index("grp") * rows + lax.axis_index("row"), 3, 2
    return jnp.where(at % 2 == m % 2, up, down)


def edge_list(sizes, lists_ref, m):
    part = lists_ref.shape[1] // 4
    at = pl.multiple_of(edge_of(sizes, m) * part, part)
    return lists_ref[:, pl.ds(at, part)]


def start_kernel(sizes, lists_ref, op_ref, u_ref, sel_ref, applied_ref, *edges):
    n = sel_ref.shape[0]
    part = n // 4
    for m in range(4):
        names = jnp.broadcast_to(edge_list(sizes, lists_ref, m), (128, part)).T
        lanes = lax.broadcasted_iota(jnp.int32, (part, 128), 1)
        for j in range(n // 128):
            hit = names == lanes + j * 128
            sel_ref[m * part : (m + 1) * part, j * 128 : (j + 1) * 128] = jnp.where(hit, 1.0, 0.0).astype(BF)
    applied = dot(op_ref[...], u_ref[...].astype(BF))
    applied_ref[...] = applied
    applied = applied.astype(BF)
    for m, edge in enumerate(edges):
        edge[...] = dot(sel_ref[m * part : (m + 1) * part, :], applied).astype(BF)


def tables_kernel(sizes, lists_ref, basis_t_ref, slot_ref, scatter_ref, based_ref, based_t_ref):
    n = scatter_ref.shape[0]
    part = n // 4
    for m in range(4):
        rows = lax.broadcasted_iota(jnp.int32, (n, part), 0)
        hit = rows == edge_list(sizes, lists_ref, m)
        scatter_ref[:, m * part : (m + 1) * part] = jnp.where(hit, 1.0, 0.0).astype(BF)
    nb = basis_t_ref.shape[0]
    pick = lax.broadcasted_iota(jnp.int32, (nb, nb), 0) == slot_ref[...]
    based_t = dot(jnp.where(pick, 1.0, 0.0).astype(BF), basis_t_ref[...])
    based_t_ref[...] = based_t.astype(BF)
    based_ref[...] = based_t.T.astype(BF)


def prepare_kernel(sel_ref, pre_ref, op_ref, based_ref, pre_sel_ref, lift_ref, lift_sel_ref):
    pre_sel_ref[...] = dot(sel_ref[...], pre_ref[...]).astype(BF)
    lift = dot(op_ref[...], based_ref[...]).astype(BF)
    lift_ref[...] = lift
    lift_sel_ref[...] = dot(sel_ref[...], lift).astype(BF)


def shared(sizes):
    grps, rows, cols = sizes
    a = lax.axis_index("grp") * rows + lax.axis_index("row")
    c = lax.axis_index("col")

    def partner(at, count, odd):
        up = at % 2 == odd
        return jnp.where(up, at + 1 < count, at > 0)

    return [
        partner(c, cols, 0),
        partner(c, cols, 1),
        partner(a, grps * rows, 0),
        partner(a, grps * rows, 1),
    ]


def resid_kernel(sizes, load_ref, applied_ref, scatter_ref, based_t_ref, n0, n1, n2, n3, resid_ref, coarse_ref, gathered):
    part = n0.shape[0]
    for m, (there, near) in enumerate(zip(shared(sizes), (n0, n1, n2, n3))):
        gathered[m * part : (m + 1) * part, :] = jnp.where(there, near[...], jnp.zeros_like(near))
    resid = load_ref[...] - applied_ref[...] - dot(scatter_ref[...], gathered[...])
    resid = resid.astype(BF)
    resid_ref[...] = resid
    coarse_ref[...] = dot(based_t_ref[...], resid).astype(BF)


def fix_kernel(pre_sel_ref, resid_ref, fix_ref, *edges):
    part = edges[0].shape[0]
    for m, edge in enumerate(edges):
        rows = slice(m * part, (m + 1) * part)
        fix = dot(pre_sel_ref[rows, :], resid_ref[...])
        fix_ref[rows, :] = fix
        edge[...] = fix.astype(BF)


def smoothed(sizes, u, fix_ref, scatter_ref, near, blended):
    part = near[0].shape[0]
    for m, there in enumerate(shared(sizes)):
        rows = slice(m * part, (m + 1) * part)
        fix = fix_ref[rows, :]
        both = 0.5 * (fix + near[m][...].astype(F32))
        blended[rows, :] = jnp.where(there, both, fix).astype(BF)
    return u + OMEGA * dot(scatter_ref[...], blended[...])


def middle_kernel(sizes, op_ref, sel_ref, u_ref, fix_ref, scatter_ref, *refs):
    near, (out_ref, applied_ref, edge_ref, blended) = refs[:4], refs[4:]
    u = smoothed(sizes, u_ref[...], fix_ref, scatter_ref, near, blended)
    out_ref[...] = u
    applied = dot(op_ref[...], u.astype(BF))
    applied_ref[...] = applied
    edge_ref[...] = dot(sel_ref[...], applied.astype(BF))


def solution_of(mine_ref, others):
    solved = mine_ref[...]
    for other in others:
        solved = solved + other[...].astype(F32)
    return solved.astype(BF)


def next_kernel(lift_ref, lift_sel_ref, applied_ref, edge_ref, mine_ref, *refs):
    others, (solved_ref, out_ref, *edges) = refs[:-6], refs[-6:]
    solved = solution_of(mine_ref, others)
    solved_ref[...] = solved
    part = edges[0].shape[0]
    for m, edge in enumerate(edges):
        rows = slice(m * part, (m + 1) * part)
        edge[...] = (edge_ref[rows, :] + OMEGA * dot(lift_sel_ref[rows, :], solved)).astype(BF)
    out_ref[...] = applied_ref[...] + OMEGA * dot(lift_ref[...], solved)


def late_kernel(sizes, u_ref, fix_ref, scatter_ref, based_ref, solved_ref, *refs):
    near, (out_ref, blended) = refs[:4], refs[4:]
    u = u_ref[...] + OMEGA * dot(based_ref[...], solved_ref[...])
    out_ref[...] = smoothed(sizes, u, fix_ref, scatter_ref, near, blended)


def last_kernel(u_ref, based_ref, mine_ref, *refs):
    others, out_ref = refs[:-1], refs[-1]
    out_ref[...] = u_ref[...] + OMEGA * dot(based_ref[...], solution_of(mine_ref, others))


def regroup_kernel(geometry, nb, inverse_ref, *blocks):
    _, ratio, lines = geometry
    c = lax.axis_index("col")
    owner = c // ratio
    for k, block in enumerate(blocks):
        target = k ^ owner
        parity, pair = target % 2, target // 2
        for line in range(lines):
            rows = pl.ds(pl.multiple_of((2 * line + parity) * nb, nb), nb)
            cols = pl.ds(pl.multiple_of(pair * 2 * nb, 2 * nb), 2 * nb)
            block[line * nb : (line + 1) * nb, :] = inverse_ref[rows, cols]


def coarse_kernel(geometry, row_size, nb, moves, *refs):
    grid_rows, _, lines = geometry
    blocks, refs = refs[:grid_rows], refs[grid_rows:]
    vectors, refs = refs[: len(moves)], refs[len(moves) :]
    mine_ref, others, (stack, total) = refs[0], refs[1:lines], refs[lines:]
    g, r, c = (lax.axis_index(axis) for axis in AXES)
    for (dg, dr, dc), vector in zip(moves, vectors):
        at = (((g ^ dg) * row_size + (r ^ dr)) * 2 + ((c % 2) ^ dc)) * nb
        stack[pl.ds(pl.multiple_of(at, nb), nb), :] = vector[...]
    acc = None
    for k, block in enumerate(blocks):
        owner = k ^ (c % grid_rows)
        part = dot(block[...], stack[pl.ds(pl.multiple_of(owner * 2 * nb, 2 * nb), 2 * nb), :])
        acc = part if acc is None else acc + part
    total[...] = acc
    line = c // 2
    for k in range(lines):
        got = total[pl.ds(pl.multiple_of((line ^ k) * nb, nb), nb), :]
        if k == 0:
            mine_ref[...] = got
        else:
            others[k - 1][...] = got.astype(BF)


def body(load, guess, interface_op, precond, basis, coarse_inverse, edge_rows, coarse_slot):
    sizes = tuple(lax.axis_size(axis) for axis in AXES)
    grps, row_size, cols = sizes
    grid_rows = grps * row_size
    load, u, op, pre = load[0, 0], guess[0, 0], interface_op[0, 0], precond[0, 0]
    basis_t = jnp.swapaxes(basis[0, 0], 0, 1)
    slot, lists = coarse_slot[0], edge_rows[0]
    n, cases = load.shape
    nb = basis_t.shape[0]
    part = n // 4
    ratio, lines = cols // grid_rows, cols // 2
    geometry = (grid_rows, ratio, lines)

    halo_pairs = [matching(sizes, m % 2, m < 2) for m in range(4)]
    far_moves = [(dr, dc) for dr in range(row_size) for dc in range(2)]
    moves = [(dg, dr, dc) for dr, dc in far_moves for dg in range(grps)]

    def swap_pairs(dg, dr, dc):
        return pairs_of(sizes, lambda g, r, c: (g ^ dg, r ^ dr, c ^ dc))

    def target(k):
        return pairs_of(sizes, lambda g, r, c: (g, r, (c % ratio) * grid_rows + (k ^ (c // ratio))))

    field = shape((n, cases), F32)
    edge = shape((part, cases), BF)
    square = shape((n, n), BF)
    thin = shape((n, nb), BF)
    vector = shape((nb, cases), BF)
    flops = 2 * n * n * cases

    def halo(edges):
        return [send(e, p) for e, p in zip(edges, halo_pairs)]

    blocks = call(
        functools.partial(regroup_kernel, geometry, nb),
        [shape((lines * nb, 2 * nb), BF)] * grid_rows,
        [coarse_inverse],
        n,
    )
    blocks = [send(block, target(k)) for k, block in enumerate(blocks)]
    sel, applied, *edges = call(
        functools.partial(start_kernel, sizes), [square, field] + [edge] * 4, [lists, op, u], 2 * flops
    )
    near = halo(edges)
    scatter, based, based_t = call(
        functools.partial(tables_kernel, sizes), [square, thin, shape((nb, n), BF)], [lists, basis_t, slot], n * n
    )
    pre_sel, lift, lift_sel = call(prepare_kernel, [square, thin, thin], [sel, pre, op, based], 2 * n * n * n)

    scratch = [pltpu.VMEM((n, cases), BF)]
    for sweep in range(ITERS):
        resid, coarse = call(
            functools.partial(resid_kernel, sizes),
            [shape((n, cases), BF), vector],
            [load, applied, scatter, based_t, *near],
            flops,
            scratch,
        )
        vectors = {}
        for dr, dc in far_moves:
            got = coarse if dr + dc == 0 else send(coarse, swap_pairs(0, dr, dc))
            vectors[0, dr, dc] = got
            for dg in range(1, grps):
                vectors[dg, dr, dc] = send(got, swap_pairs(dg, 0, 0))
        fix, *own = call(fix_kernel, [field] + [edge] * 4, [pre_sel, resid], flops)
        near = halo(own)
        mine, *others = call(
            functools.partial(coarse_kernel, geometry, row_size, nb, moves),
            [shape((nb, cases), F32)] + [vector] * (lines - 1),
            [*blocks, *(vectors[move] for move in moves)],
            2 * lines * nb * 2 * nb * grid_rows * cases,
            [pltpu.VMEM((2 * grid_rows * nb, cases), BF), pltpu.VMEM((lines * nb, cases), F32)],
        )
        others = [send(o, swap_pairs(0, 0, 2 * (k + 1))) for k, o in enumerate(others)]
        if sweep < ITERS - 1:
            inputs = [u, fix, scatter, *near]
            u, applied, edge_part = call(
                functools.partial(middle_kernel, sizes), [field] * 3, [op, sel, *inputs], 3 * flops, scratch
            )
            solved, applied, *edges = call(
                next_kernel,
                [vector, field] + [edge] * 4,
                [lift, lift_sel, applied, edge_part, mine, *others],
                n * nb * cases,
            )
            near = halo(edges)
        else:
            u = call(
                functools.partial(late_kernel, sizes), field, [u, fix, scatter, based, solved, *near], flops, scratch
            )
            u = call(last_kernel, field, [u, based, mine, *others], n * nb * cases)
    return u[None, None]


def solution(mesh):
    cells = P(("grp", "row"), "col", None, None)
    lists = P(("grp", "row"), "col", None)

    return jax.shard_map(
        body,
        mesh=mesh,
        in_specs=(cells, cells, cells, cells, cells, P(("grp", "row"), "col"), lists, lists),
        out_specs=cells,
        check_vma=False,
    )
```

```python
import functools

import jax
import jax.numpy as jnp
from jax import lax
from jax.experimental import pallas as pl
from jax.experimental.pallas import tpu as pltpu
from jax.sharding import PartitionSpec as P


ITERS = 2
OMEGA = 0.6
AXES = ("grp", "row", "col")
BF = jnp.bfloat16
F32 = jnp.float32
VMEM_LIMIT = 24 << 20
CHUNKS = 4


def dot(a, b):
    return jnp.dot(a, b, preferred_element_type=F32)


def call(kernel, outs, args, flops, scratch=(), far=(), far_out=False):
    moved = sum(a.size * a.dtype.itemsize for a in args)
    vmem, hbm = pl.BlockSpec(memory_space=pltpu.VMEM), pl.BlockSpec(memory_space=pltpu.HBM)
    out_spec = hbm if far_out else vmem
    return pl.pallas_call(
        kernel,
        out_shape=outs,
        in_specs=[hbm if k in far else vmem for k in range(len(args))],
        out_specs=[out_spec] * len(outs) if isinstance(outs, list) else out_spec,
        scratch_shapes=list(scratch),
        compiler_params=pltpu.CompilerParams(vmem_limit_bytes=VMEM_LIMIT),
        cost_estimate=pl.CostEstimate(flops=flops, transcendentals=0, bytes_accessed=moved),
    )(*args)


def chunk_copies(source, target, sems, first, count):
    rows = source.shape[0] // count
    return [
        pltpu.make_async_copy(
            source.at[pl.ds(k * rows, rows)], target.at[pl.ds(k * rows, rows)], sems.at[first + k]
        )
        for k in range(count)
    ]


def shape(dims, dtype):
    return jax.ShapeDtypeStruct(tuple(dims), dtype)


def pairs_of(sizes, where):
    grps, rows, cols = sizes
    flat = lambda g, r, c: (g * rows + r) * cols + c
    return [
        (flat(g, r, c), flat(*where(g, r, c)))
        for g in range(grps)
        for r in range(rows)
        for c in range(cols)
    ]


def matching(sizes, odd, along_cols):
    grps, rows, cols = sizes
    count = cols if along_cols else grps * rows

    def where(g, r, c):
        at = c if along_cols else g * rows + r
        to = at + 1 if at % 2 == odd else at - 1
        if 0 <= to < count:
            return (g, r, to) if along_cols else (to // rows, to % rows, c)
        if along_cols and grps == 2:
            return (1 - g, r, c)
        if not along_cols and cols % 4 == 0:
            return (g, r, c ^ 2)
        return (g, r, c)

    return pairs_of(sizes, where)


def send(value, pairs):
    return lax.ppermute(value, AXES, pairs)


def edge_of(sizes, m):
    _, rows, _ = sizes
    if m < 2:
        at, up, down = lax.axis_index("col"), 1, 0
    else:
        at, up, down = lax.axis_index("grp") * rows + lax.axis_index("row"), 3, 2
    return jnp.where(at % 2 == m % 2, up, down)


def edge_list(sizes, lists_ref, m):
    part = lists_ref.shape[1] // 4
    at = pl.multiple_of(edge_of(sizes, m) * part, part)
    return lists_ref[:, pl.ds(at, part)]


def start_kernel(sizes, lists_ref, op_hbm, u_hbm, sel_ref, op_ref, u_ref, applied_ref, *refs):
    edges, sems = refs[:-1], refs[-1]
    u_copies = chunk_copies(u_hbm, u_ref, sems, 0, CHUNKS)
    op_copies = chunk_copies(op_hbm, op_ref, sems, CHUNKS, CHUNKS)
    for copy in u_copies + op_copies:
        copy.start()
    n = sel_ref.shape[0]
    part = n // 4
    for m in range(4):
        names = jnp.broadcast_to(edge_list(sizes, lists_ref, m), (128, part)).T
        lanes = lax.broadcasted_iota(jnp.int32, (part, 128), 1)
        for j in range(n // 128):
            hit = names == lanes + j * 128
            sel_ref[m * part : (m + 1) * part, j * 128 : (j + 1) * 128] = jnp.where(hit, 1.0, 0.0).astype(BF)
    for copy in u_copies:
        copy.wait()
    u = u_ref[...].astype(BF)
    rows = n // CHUNKS
    for k, copy in enumerate(op_copies):
        copy.wait()
        applied_ref[k * rows : (k + 1) * rows, :] = dot(op_ref[k * rows : (k + 1) * rows, :], u)
    applied = applied_ref[...].astype(BF)
    for m, edge in enumerate(edges):
        edge[...] = dot(sel_ref[m * part : (m + 1) * part, :], applied).astype(BF)


def tables_kernel(
    sizes, lists_ref, basis_t_ref, slot_ref, sel_ref, pre_hbm, load_hbm,
    scatter_ref, based_ref, based_t_ref, pre_sel_ref, load_ref, pre_ref, sems,
):
    copies = chunk_copies(pre_hbm, pre_ref, sems, 0, CHUNKS) + chunk_copies(load_hbm, load_ref, sems, CHUNKS, CHUNKS)
    for copy in copies:
        copy.start()
    n = scatter_ref.shape[0]
    part = n // 4
    for m in range(4):
        rows = lax.broadcasted_iota(jnp.int32, (n, part), 0)
        hit = rows == edge_list(sizes, lists_ref, m)
        scatter_ref[:, m * part : (m + 1) * part] = jnp.where(hit, 1.0, 0.0).astype(BF)
    nb = basis_t_ref.shape[0]
    pick = lax.broadcasted_iota(jnp.int32, (nb, nb), 0) == slot_ref[...]
    based_t = dot(jnp.where(pick, 1.0, 0.0).astype(BF), basis_t_ref[...])
    based_t_ref[...] = based_t.astype(BF)
    based_ref[...] = based_t.T.astype(BF)
    for copy in copies:
        copy.wait()
    pre_sel_ref[...] = dot(sel_ref[...], pre_ref[...]).astype(BF)


def lift_kernel(sel_ref, op_ref, based_ref, lift_ref, lift_sel_ref):
    lift = dot(op_ref[...], based_ref[...]).astype(BF)
    lift_ref[...] = lift
    lift_sel_ref[...] = dot(sel_ref[...], lift).astype(BF)


def shared(sizes):
    grps, rows, cols = sizes
    a = lax.axis_index("grp") * rows + lax.axis_index("row")
    c = lax.axis_index("col")

    def partner(at, count, odd):
        up = at % 2 == odd
        return jnp.where(up, at + 1 < count, at > 0)

    return [
        partner(c, cols, 0),
        partner(c, cols, 1),
        partner(a, grps * rows, 0),
        partner(a, grps * rows, 1),
    ]


def resid_kernel(sizes, load_ref, applied_ref, scatter_ref, based_t_ref, n0, n1, n2, n3, resid_ref, coarse_ref, gathered):
    part = n0.shape[0]
    for m, (there, near) in enumerate(zip(shared(sizes), (n0, n1, n2, n3))):
        gathered[m * part : (m + 1) * part, :] = jnp.where(there, near[...], jnp.zeros_like(near))
    resid = load_ref[...] - applied_ref[...] - dot(scatter_ref[...], gathered[...])
    resid = resid.astype(BF)
    resid_ref[...] = resid
    coarse_ref[...] = dot(based_t_ref[...], resid).astype(BF)


def fix_kernel(pre_sel_ref, resid_ref, fix_ref, *edges):
    part = edges[0].shape[0]
    for m, edge in enumerate(edges):
        rows = slice(m * part, (m + 1) * part)
        fix = dot(pre_sel_ref[rows, :], resid_ref[...])
        fix_ref[rows, :] = fix
        edge[...] = fix.astype(BF)


def smoothed(sizes, u, fix_ref, scatter_ref, near, blended):
    part = near[0].shape[0]
    for m, there in enumerate(shared(sizes)):
        rows = slice(m * part, (m + 1) * part)
        fix = fix_ref[rows, :]
        both = 0.5 * (fix + near[m][...].astype(F32))
        blended[rows, :] = jnp.where(there, both, fix).astype(BF)
    return u + OMEGA * dot(scatter_ref[...], blended[...])


def middle_kernel(sizes, op_ref, sel_ref, u_ref, fix_ref, scatter_ref, *refs):
    near, (out_ref, applied_ref, edge_ref, blended) = refs[:4], refs[4:]
    u = smoothed(sizes, u_ref[...], fix_ref, scatter_ref, near, blended)
    out_ref[...] = u
    applied = dot(op_ref[...], u.astype(BF))
    applied_ref[...] = applied
    edge_ref[...] = dot(sel_ref[...], applied.astype(BF))


def solution_of(mine_ref, others):
    solved = mine_ref[...]
    for other in others:
        solved = solved + other[...].astype(F32)
    return solved.astype(BF)


def next_kernel(lift_ref, lift_sel_ref, applied_ref, edge_ref, mine_ref, *refs):
    others, (solved_ref, out_ref, *edges) = refs[:-6], refs[-6:]
    solved = solution_of(mine_ref, others)
    solved_ref[...] = solved
    part = edges[0].shape[0]
    for m, edge in enumerate(edges):
        rows = slice(m * part, (m + 1) * part)
        edge[...] = (edge_ref[rows, :] + OMEGA * dot(lift_sel_ref[rows, :], solved)).astype(BF)
    out_ref[...] = applied_ref[...] + OMEGA * dot(lift_ref[...], solved)


def late_kernel(sizes, u_ref, fix_ref, scatter_ref, based_ref, solved_ref, *refs):
    near, (out_ref, blended) = refs[:4], refs[4:]
    u = u_ref[...] + OMEGA * dot(based_ref[...], solved_ref[...])
    out_ref[...] = smoothed(sizes, u, fix_ref, scatter_ref, near, blended)


def last_kernel(u_ref, based_ref, mine_ref, *refs):
    others, (out_hbm, total, sems) = refs[:-3], refs[-3:]
    solved = solution_of(mine_ref, others)
    copies = chunk_copies(total, out_hbm, sems, 0, CHUNKS)
    rows = total.shape[0] // CHUNKS
    for k, copy in enumerate(copies):
        at = slice(k * rows, (k + 1) * rows)
        total[at, :] = u_ref[at, :] + OMEGA * dot(based_ref[at, :], solved)
        copy.start()
    for copy in copies:
        copy.wait()


def regroup_kernel(geometry, nb, inverse_ref, *blocks):
    _, ratio, lines = geometry
    c = lax.axis_index("col")
    owner = c // ratio
    for k, block in enumerate(blocks):
        target = k ^ owner
        parity, pair = target % 2, target // 2
        for line in range(lines):
            rows = pl.ds(pl.multiple_of((2 * line + parity) * nb, nb), nb)
            cols = pl.ds(pl.multiple_of(pair * 2 * nb, 2 * nb), 2 * nb)
            block[line * nb : (line + 1) * nb, :] = inverse_ref[rows, cols]


def split_kernel(nb, inverse_hbm, keep_ref, give_ref, sems):
    parity = lax.axis_index("col") % 2
    copies = []
    for line in range(keep_ref.shape[0] // nb):
        for k, (ref, mine) in enumerate(((keep_ref, parity), (give_ref, 1 - parity))):
            rows = pl.ds(pl.multiple_of((2 * line + mine) * nb, nb), nb)
            copies.append(
                pltpu.make_async_copy(inverse_hbm.at[rows], ref.at[pl.ds(line * nb, nb)], sems.at[2 * line + k])
            )
    for copy in copies:
        copy.start()
    for copy in copies:
        copy.wait()


def upper_kernel(top, mine_ref, got_ref, keep_ref, give_ref):
    c = lax.axis_index("col")
    same = c % 2 == c // top
    keep_ref[...] = jnp.where(same, mine_ref[...], got_ref[...])
    give_ref[...] = jnp.where(same, got_ref[...], mine_ref[...])


def lower_kernel(first_ref, second_ref, keep_ref, give_ref):
    low = (lax.axis_index("col") // 2) % 2
    half = first_ref.shape[1] // 2
    for k, source in enumerate((first_ref, second_ref)):
        left, right = source[:, :half], source[:, half:]
        keep_ref[:, k * half : (k + 1) * half] = jnp.where(low == 0, left, right)
        give_ref[:, k * half : (k + 1) * half] = jnp.where(low == 0, right, left)


def coarse_kernel(stepwise, geometry, row_size, nb, moves, *refs):
    grid_rows, _, lines = geometry
    width = 2 * nb
    count = 2 if stepwise else grid_rows
    arrays, refs = refs[:count], refs[count:]
    vectors, refs = refs[: len(moves)], refs[len(moves) :]
    mine_ref, others, (stack, total) = refs[0], refs[1:lines], refs[lines:]
    g, r, c = (lax.axis_index(axis) for axis in AXES)
    line = c // 2
    for (dg, dr, dc), vector in zip(moves, vectors):
        at = (((g ^ dg) * row_size + (r ^ dr)) * 2 + ((c % 2) ^ dc)) * nb
        stack[pl.ds(pl.multiple_of(at, nb), nb), :] = vector[...]
    if stepwise:
        blocks = [
            (arrays[k // 2][:, (k % 2) * width : (k % 2 + 1) * width], line ^ (2 * (k % 2) + k // 2)) for k in range(4)
        ]
    else:
        blocks = [(array[...], k ^ (c % grid_rows)) for k, array in enumerate(arrays)]
    acc = None
    for block, owner in blocks:
        part = dot(block, stack[pl.ds(pl.multiple_of(owner * width, width), width), :])
        acc = part if acc is None else acc + part
    total[...] = acc
    for k in range(lines):
        got = total[pl.ds(pl.multiple_of((line ^ k) * nb, nb), nb), :]
        if k == 0:
            mine_ref[...] = got
        else:
            others[k - 1][...] = got.astype(BF)


def in_steps(sizes):
    grps, row_size, cols = sizes
    return grps * row_size == 4 and cols == 2 * grps * row_size


def body(load, guess, interface_op, precond, basis, coarse_inverse, edge_rows, coarse_slot):
    sizes = tuple(lax.axis_size(axis) for axis in AXES)
    grps, row_size, cols = sizes
    grid_rows = grps * row_size
    load, u, op, pre = load[0, 0], guess[0, 0], interface_op[0, 0], precond[0, 0]
    basis_t = jnp.swapaxes(basis[0, 0], 0, 1)
    slot, lists = coarse_slot[0], edge_rows[0]
    n, cases = load.shape
    nb = basis_t.shape[0]
    part = n // 4
    ratio, lines = cols // grid_rows, cols // 2
    geometry = (grid_rows, ratio, lines)

    halo_pairs = [matching(sizes, m % 2, m < 2) for m in range(4)]
    far_moves = [(dr, dc) for dr in range(row_size) for dc in range(2)]
    moves = [(dg, dr, dc) for dr, dc in far_moves for dg in range(grps)]

    def swap_pairs(dg, dr, dc):
        return pairs_of(sizes, lambda g, r, c: (g ^ dg, r ^ dr, c ^ dc))

    def target(k):
        return pairs_of(sizes, lambda g, r, c: (g, r, (c % ratio) * grid_rows + (k ^ (c // ratio))))

    field = shape((n, cases), F32)
    edge = shape((part, cases), BF)
    square = shape((n, n), BF)
    thin = shape((n, nb), BF)
    vector = shape((nb, cases), BF)
    flops = 2 * n * n * cases

    def halo(edges):
        return [send(e, p) for e, p in zip(edges, halo_pairs)]

    stepwise = in_steps(sizes)
    if stepwise:
        half = shape((lines * nb, coarse_inverse.shape[1]), BF)
        keep, give = call(
            functools.partial(split_kernel, nb),
            [half, half],
            [coarse_inverse],
            n,
            [pltpu.SemaphoreType.DMA((2 * lines,))],
            far=(0,),
        )
        got = send(give, swap_pairs(0, 0, 1))
    else:
        blocks = call(
            functools.partial(regroup_kernel, geometry, nb),
            [shape((lines * nb, 2 * nb), BF)] * grid_rows,
            [coarse_inverse],
            n,
        )
        blocks = [send(block, target(k)) for k, block in enumerate(blocks)]
    sems = pltpu.SemaphoreType.DMA((2 * CHUNKS,))
    sel, op, u, applied, *edges = call(
        functools.partial(start_kernel, sizes),
        [square, square, field, field] + [edge] * 4,
        [lists, op, u],
        2 * flops,
        [sems],
        far=(1, 2),
    )
    near = halo(edges)
    if stepwise:
        keep, give = call(functools.partial(upper_kernel, cols // 2), [half, half], [keep, got], n)
        got = send(give, swap_pairs(0, 0, cols // 2))
    scatter, based, based_t, pre_sel, load = call(
        functools.partial(tables_kernel, sizes),
        [square, thin, shape((nb, n), BF), square, field],
        [lists, basis_t, slot, sel, pre, load],
        2 * n * n * n,
        [pltpu.VMEM((n, n), BF), sems],
        far=(4, 5),
    )
    if stepwise:
        keep, give = call(lower_kernel, [half, half], [keep, got], n)
        blocks = [keep, send(give, swap_pairs(0, 0, 2))]

    scratch = [pltpu.VMEM((n, cases), BF)]
    for sweep in range(ITERS):
        resid, coarse = call(
            functools.partial(resid_kernel, sizes),
            [shape((n, cases), BF), vector],
            [load, applied, scatter, based_t, *near],
            flops,
            scratch,
        )
        vectors = {}
        for dr, dc in far_moves:
            got = coarse if dr + dc == 0 else send(coarse, swap_pairs(0, dr, dc))
            vectors[0, dr, dc] = got
            for dg in range(1, grps):
                vectors[dg, dr, dc] = send(got, swap_pairs(dg, 0, 0))
        fix, *own = call(fix_kernel, [field] + [edge] * 4, [pre_sel, resid], flops)
        near = halo(own)
        mine, *others = call(
            functools.partial(coarse_kernel, stepwise, geometry, row_size, nb, moves),
            [shape((nb, cases), F32)] + [vector] * (lines - 1),
            [*blocks, *(vectors[move] for move in moves)],
            2 * lines * nb * 2 * nb * grid_rows * cases,
            [pltpu.VMEM((2 * grid_rows * nb, cases), BF), pltpu.VMEM((lines * nb, cases), F32)],
        )
        others = [send(o, swap_pairs(0, 0, 2 * (k + 1))) for k, o in enumerate(others)]
        if sweep < ITERS - 1:
            lift, lift_sel = call(lift_kernel, [thin, thin], [sel, op, based], n * n * nb)
            inputs = [u, fix, scatter, *near]
            u, applied, edge_part = call(
                functools.partial(middle_kernel, sizes), [field] * 3, [op, sel, *inputs], 3 * flops, scratch
            )
            solved, applied, *edges = call(
                next_kernel,
                [vector, field] + [edge] * 4,
                [lift, lift_sel, applied, edge_part, mine, *others],
                n * nb * cases,
            )
            near = halo(edges)
        else:
            u = call(
                functools.partial(late_kernel, sizes), field, [u, fix, scatter, based, solved, *near], flops, scratch
            )
            u = call(
                last_kernel,
                field,
                [u, based, mine, *others],
                n * nb * cases,
                [pltpu.VMEM((n, cases), F32), pltpu.SemaphoreType.DMA((CHUNKS,))],
                far_out=True,
            )
    return u[None, None]


def solution(mesh):
    cells = P(("grp", "row"), "col", None, None)
    lists = P(("grp", "row"), "col", None)

    return jax.shard_map(
        body,
        mesh=mesh,
        in_specs=(cells, cells, cells, cells, cells, P(("grp", "row"), "col"), lists, lists),
        out_specs=cells,
        check_vma=False,
    )
```

```python
import functools

import jax
import jax.numpy as jnp
from jax import lax
from jax.experimental import pallas as pl
from jax.experimental.pallas import tpu as pltpu
from jax.sharding import PartitionSpec as P


ITERS = 2
OMEGA = 0.6
AXES = ("grp", "row", "col")
BF = jnp.bfloat16
F32 = jnp.float32
VMEM_LIMIT = 24 << 20
CHUNKS = 4


def dot(a, b):
    return jnp.dot(a, b, preferred_element_type=F32)


def call(kernel, outs, args, flops, scratch=(), far=(), far_out=False):
    moved = sum(a.size * a.dtype.itemsize for a in args)
    vmem, hbm = pl.BlockSpec(memory_space=pltpu.VMEM), pl.BlockSpec(memory_space=pltpu.HBM)
    out_spec = hbm if far_out else vmem
    args = [pltpu.with_memory_space_constraint(a, pltpu.HBM) if k in far else a for k, a in enumerate(args)]
    return pl.pallas_call(
        kernel,
        out_shape=outs,
        in_specs=[hbm if k in far else vmem for k in range(len(args))],
        out_specs=[out_spec] * len(outs) if isinstance(outs, list) else out_spec,
        scratch_shapes=list(scratch),
        compiler_params=pltpu.CompilerParams(vmem_limit_bytes=VMEM_LIMIT),
        cost_estimate=pl.CostEstimate(flops=flops, transcendentals=0, bytes_accessed=moved),
    )(*args)


def chunk_copies(source, target, sems, first, count):
    rows = source.shape[0] // count
    return [
        pltpu.make_async_copy(
            source.at[pl.ds(k * rows, rows)], target.at[pl.ds(k * rows, rows)], sems.at[first + k]
        )
        for k in range(count)
    ]


def shape(dims, dtype):
    return jax.ShapeDtypeStruct(tuple(dims), dtype)


def pairs_of(sizes, where):
    grps, rows, cols = sizes
    flat = lambda g, r, c: (g * rows + r) * cols + c
    return [
        (flat(g, r, c), flat(*where(g, r, c)))
        for g in range(grps)
        for r in range(rows)
        for c in range(cols)
    ]


def matching(sizes, odd, along_cols):
    grps, rows, cols = sizes
    count = cols if along_cols else grps * rows

    def where(g, r, c):
        at = c if along_cols else g * rows + r
        to = at + 1 if at % 2 == odd else at - 1
        if 0 <= to < count:
            return (g, r, to) if along_cols else (to // rows, to % rows, c)
        if along_cols and grps == 2:
            return (1 - g, r, c)
        if not along_cols and cols % 4 == 0:
            return (g, r, c ^ 2)
        return (g, r, c)

    return pairs_of(sizes, where)


def send(value, pairs):
    return lax.ppermute(value, AXES, pairs)


def edge_of(sizes, m):
    _, rows, _ = sizes
    if m < 2:
        at, up, down = lax.axis_index("col"), 1, 0
    else:
        at, up, down = lax.axis_index("grp") * rows + lax.axis_index("row"), 3, 2
    return jnp.where(at % 2 == m % 2, up, down)


def edge_list(sizes, lists_ref, m):
    part = lists_ref.shape[1] // 4
    at = pl.multiple_of(edge_of(sizes, m) * part, part)
    return lists_ref[:, pl.ds(at, part)]


def load_kernel(sizes, nb, lists_hbm, op_hbm, u_hbm, *refs):
    if len(refs) > 5:
        inverse_hbm, lists_ref, sel_ref, op_ref, u_ref, keep_ref, give_ref, sems = refs
    else:
        lists_ref, sel_ref, op_ref, u_ref, sems = refs
    named = pltpu.make_async_copy(lists_hbm, lists_ref, sems.at[0])
    copies = []
    if len(refs) > 5:
        parity = lax.axis_index("col") % 2
        lines = keep_ref.shape[0] // nb
        for line in range(lines):
            for k, (ref, mine) in enumerate(((keep_ref, parity), (give_ref, 1 - parity))):
                rows = pl.ds(pl.multiple_of((2 * line + mine) * nb, nb), nb)
                sem = sems.at[1 + 2 * CHUNKS + 2 * line + k]
                copies.append(pltpu.make_async_copy(inverse_hbm.at[rows], ref.at[pl.ds(line * nb, nb)], sem))
    copies += chunk_copies(u_hbm, u_ref, sems, 1, CHUNKS)
    copies += chunk_copies(op_hbm, op_ref, sems, 1 + CHUNKS, CHUNKS)
    for copy in [named] + copies:
        copy.start()
    named.wait()
    n = sel_ref.shape[0]
    part = n // 4
    for m in range(4):
        names = jnp.broadcast_to(edge_list(sizes, lists_ref, m), (128, part)).T
        lanes = lax.broadcasted_iota(jnp.int32, (part, 128), 1)
        for j in range(n // 128):
            hit = names == lanes + j * 128
            sel_ref[m * part : (m + 1) * part, j * 128 : (j + 1) * 128] = jnp.where(hit, 1.0, 0.0).astype(BF)
    for copy in copies:
        copy.wait()


def apply_kernel(op_ref, u_ref, sel_ref, applied_ref, *edges):
    applied = dot(op_ref[...], u_ref[...].astype(BF))
    applied_ref[...] = applied
    split_edges(applied, sel_ref, edges)


def split_edges(field, sel_ref, edges):
    field = field.astype(BF)
    part = edges[0].shape[0]
    for m, edge in enumerate(edges):
        edge[...] = dot(sel_ref[m * part : (m + 1) * part, :], field).astype(BF)


def tables_kernel(sizes, lists_ref, basis_t_ref, slot_ref, scatter_ref, based_ref, based_t_ref):
    n = scatter_ref.shape[0]
    part = n // 4
    for m in range(4):
        rows = lax.broadcasted_iota(jnp.int32, (n, part), 0)
        hit = rows == edge_list(sizes, lists_ref, m)
        scatter_ref[:, m * part : (m + 1) * part] = jnp.where(hit, 1.0, 0.0).astype(BF)
    nb = basis_t_ref.shape[0]
    pick = lax.broadcasted_iota(jnp.int32, (nb, nb), 0) == slot_ref[...]
    based_t = dot(jnp.where(pick, 1.0, 0.0).astype(BF), basis_t_ref[...])
    based_t_ref[...] = based_t.astype(BF)
    based_ref[...] = based_t.T.astype(BF)


def product_kernel(left_ref, right_ref, out_ref):
    out_ref[...] = dot(left_ref[...], right_ref[...]).astype(BF)


def shared(sizes):
    grps, rows, cols = sizes
    a = lax.axis_index("grp") * rows + lax.axis_index("row")
    c = lax.axis_index("col")

    def partner(at, count, odd):
        up = at % 2 == odd
        return jnp.where(up, at + 1 < count, at > 0)

    return [
        partner(c, cols, 0),
        partner(c, cols, 1),
        partner(a, grps * rows, 0),
        partner(a, grps * rows, 1),
    ]


def scattered(sizes, scatter_ref, near, which):
    part = near[0].shape[0]
    there = shared(sizes)
    total = None
    for m, got in zip(which, near):
        got = jnp.where(there[m], got[...], jnp.zeros_like(got))
        add = dot(scatter_ref[:, m * part : (m + 1) * part], got)
        total = add if total is None else total + add
    return total


def early_kernel(sizes, load_ref, applied_ref, scatter_ref, n0, n2, out_ref):
    out_ref[...] = load_ref[...] - applied_ref[...] - scattered(sizes, scatter_ref, (n0, n2), (0, 2))


def resid_kernel(sizes, early_ref, scatter_ref, based_t_ref, n1, n3, resid_ref, coarse_ref):
    resid = (early_ref[...] - scattered(sizes, scatter_ref, (n1, n3), (1, 3))).astype(BF)
    resid_ref[...] = resid
    coarse_ref[...] = dot(based_t_ref[...], resid).astype(BF)


def fix_plain_kernel(pre_ref, sel_ref, resid_ref, fix_ref, *edges):
    fix = dot(pre_ref[...], resid_ref[...]).astype(BF)
    part = edges[0].shape[0]
    for m, edge in enumerate(edges):
        rows = slice(m * part, (m + 1) * part)
        own = dot(sel_ref[rows, :], fix)
        fix_ref[rows, :] = own
        edge[...] = own.astype(BF)


def fix_kernel(pre_sel_ref, resid_ref, fix_ref, *edges):
    part = edges[0].shape[0]
    for m, edge in enumerate(edges):
        rows = slice(m * part, (m + 1) * part)
        fix = dot(pre_sel_ref[rows, :], resid_ref[...])
        fix_ref[rows, :] = fix
        edge[...] = fix.astype(BF)


def smoothed(sizes, u, fix_ref, scatter_ref, near, blended):
    part = near[0].shape[0]
    for m, there in enumerate(shared(sizes)):
        rows = slice(m * part, (m + 1) * part)
        fix = fix_ref[rows, :]
        both = 0.5 * (fix + near[m][...].astype(F32))
        blended[rows, :] = jnp.where(there, both, fix).astype(BF)
    return u + OMEGA * dot(scatter_ref[...], blended[...])


def middle_kernel(sizes, op_ref, u_ref, fix_ref, scatter_ref, *refs):
    near, (out_ref, applied_ref, blended) = refs[:4], refs[4:]
    u = smoothed(sizes, u_ref[...], fix_ref, scatter_ref, near, blended)
    out_ref[...] = u
    applied_ref[...] = dot(op_ref[...], u.astype(BF))


def solution_of(mine_ref, others):
    solved = mine_ref[...]
    for other in others:
        solved = solved + other[...].astype(F32)
    return solved.astype(BF)


def next_kernel(lift_ref, sel_ref, applied_ref, mine_ref, *refs):
    others, (solved_ref, out_ref, *edges) = refs[:-6], refs[-6:]
    solved = solution_of(mine_ref, others)
    solved_ref[...] = solved
    applied = applied_ref[...] + OMEGA * dot(lift_ref[...], solved)
    out_ref[...] = applied
    split_edges(applied, sel_ref, edges)


def late_kernel(sizes, u_ref, fix_ref, scatter_ref, based_ref, solved_ref, *refs):
    near, (out_ref, blended) = refs[:4], refs[4:]
    u = u_ref[...] + OMEGA * dot(based_ref[...], solved_ref[...])
    out_ref[...] = smoothed(sizes, u, fix_ref, scatter_ref, near, blended)


def last_kernel(u_ref, based_ref, mine_ref, *refs):
    others, (out_hbm, total, sems) = refs[:-3], refs[-3:]
    solved = solution_of(mine_ref, others)
    copies = chunk_copies(total, out_hbm, sems, 0, CHUNKS)
    rows = total.shape[0] // CHUNKS
    for k, copy in enumerate(copies):
        at = slice(k * rows, (k + 1) * rows)
        total[at, :] = u_ref[at, :] + OMEGA * dot(based_ref[at, :], solved)
        copy.start()
    for copy in copies:
        copy.wait()


def regroup_kernel(geometry, nb, inverse_ref, *blocks):
    _, ratio, lines = geometry
    c = lax.axis_index("col")
    owner = c // ratio
    for k, block in enumerate(blocks):
        target = k ^ owner
        parity, pair = target % 2, target // 2
        for line in range(lines):
            rows = pl.ds(pl.multiple_of((2 * line + parity) * nb, nb), nb)
            cols = pl.ds(pl.multiple_of(pair * 2 * nb, 2 * nb), 2 * nb)
            block[line * nb : (line + 1) * nb, :] = inverse_ref[rows, cols]


def upper_kernel(top, mine_ref, got_ref, keep_ref, give_ref):
    c = lax.axis_index("col")
    same = c % 2 == c // top
    keep_ref[...] = jnp.where(same, mine_ref[...], got_ref[...])
    give_ref[...] = jnp.where(same, got_ref[...], mine_ref[...])


def lower_kernel(first_ref, second_ref, keep_ref, give_ref):
    low = (lax.axis_index("col") // 2) % 2
    half = first_ref.shape[1] // 2
    for k, source in enumerate((first_ref, second_ref)):
        left, right = source[:, :half], source[:, half:]
        keep_ref[:, k * half : (k + 1) * half] = jnp.where(low == 0, left, right)
        give_ref[:, k * half : (k + 1) * half] = jnp.where(low == 0, right, left)


def coarse_kernel(stepwise, geometry, row_size, nb, moves, *refs):
    grid_rows, _, lines = geometry
    width = 2 * nb
    count = 2 if stepwise else grid_rows
    arrays, refs = refs[:count], refs[count:]
    vectors, refs = refs[: len(moves)], refs[len(moves) :]
    mine_ref, others, (stack, total) = refs[0], refs[1:lines], refs[lines:]
    g, r, c = (lax.axis_index(axis) for axis in AXES)
    line = c // 2
    for (dg, dr, dc), vector in zip(moves, vectors):
        at = (((g ^ dg) * row_size + (r ^ dr)) * 2 + ((c % 2) ^ dc)) * nb
        stack[pl.ds(pl.multiple_of(at, nb), nb), :] = vector[...]
    if stepwise:
        blocks = [
            (arrays[k // 2][:, (k % 2) * width : (k % 2 + 1) * width], line ^ (2 * (k % 2) + k // 2)) for k in range(4)
        ]
    else:
        blocks = [(array[...], k ^ (c % grid_rows)) for k, array in enumerate(arrays)]
    acc = None
    for block, owner in blocks:
        part = dot(block, stack[pl.ds(pl.multiple_of(owner * width, width), width), :])
        acc = part if acc is None else acc + part
    total[...] = acc
    for k in range(lines):
        got = total[pl.ds(pl.multiple_of((line ^ k) * nb, nb), nb), :]
        if k == 0:
            mine_ref[...] = got
        else:
            others[k - 1][...] = got.astype(BF)


def in_steps(sizes):
    grps, row_size, cols = sizes
    return grps * row_size == 4 and cols == 2 * grps * row_size


def body(load, guess, interface_op, precond, basis, coarse_inverse, edge_rows, coarse_slot):
    sizes = tuple(lax.axis_size(axis) for axis in AXES)
    grps, row_size, cols = sizes
    grid_rows = grps * row_size
    load, u, op, pre = load[0, 0], guess[0, 0], interface_op[0, 0], precond[0, 0]
    basis_t = jnp.swapaxes(basis[0, 0], 0, 1)
    slot, lists = coarse_slot[0], edge_rows[0]
    n, cases = load.shape
    nb = basis_t.shape[0]
    part = n // 4
    ratio, lines = cols // grid_rows, cols // 2
    geometry = (grid_rows, ratio, lines)

    halo_pairs = [matching(sizes, m % 2, m < 2) for m in range(4)]
    far_moves = [(dr, dc) for dr in range(row_size) for dc in range(2)]
    moves = [(dg, dr, dc) for dr, dc in far_moves for dg in range(grps)]

    def swap_pairs(dg, dr, dc):
        return pairs_of(sizes, lambda g, r, c: (g ^ dg, r ^ dr, c ^ dc))

    def target(k):
        return pairs_of(sizes, lambda g, r, c: (g, r, (c % ratio) * grid_rows + (k ^ (c // ratio))))

    field = shape((n, cases), F32)
    edge = shape((part, cases), BF)
    square = shape((n, n), BF)
    thin = shape((n, nb), BF)
    vector = shape((nb, cases), BF)
    flops = 2 * n * n * cases

    def halo(edges):
        return [send(e, p) for e, p in zip(edges, halo_pairs)]

    stepwise = in_steps(sizes)
    half = shape((lines * nb, coarse_inverse.shape[1]), BF)
    lists, sel, op, u, *halves = call(
        functools.partial(load_kernel, sizes, nb),
        [shape(lists.shape, lists.dtype), square, square, field] + [half, half] * stepwise,
        [lists, op, u] + [coarse_inverse] * stepwise,
        n * n,
        [pltpu.SemaphoreType.DMA((1 + 2 * CHUNKS + 2 * lines,))],
        far=(0, 1, 2, 3),
    )
    if stepwise:
        keep, give = halves
        got = send(give, swap_pairs(0, 0, 1))
    else:
        blocks = call(
            functools.partial(regroup_kernel, geometry, nb),
            [shape((lines * nb, 2 * nb), BF)] * grid_rows,
            [coarse_inverse],
            n,
        )
        blocks = [send(block, target(k)) for k, block in enumerate(blocks)]
    applied, *edges = call(apply_kernel, [field] + [edge] * 4, [op, u, sel], 2 * flops)
    near = halo(edges)
    if stepwise:
        keep, give = call(functools.partial(upper_kernel, cols // 2), [half, half], [keep, got], n)
        got = send(give, swap_pairs(0, 0, cols // 2))
    scatter, based, based_t = call(
        functools.partial(tables_kernel, sizes), [square, thin, shape((nb, n), BF)], [lists, basis_t, slot], n * n
    )
    if stepwise:
        keep, give = call(lower_kernel, [half, half], [keep, got], n)
        blocks = [keep, send(give, swap_pairs(0, 0, 2))]

    scratch = [pltpu.VMEM((n, cases), BF)]
    for sweep in range(ITERS):
        if sweep == 1:
            pre_sel = call(product_kernel, square, [sel, pre], 2 * n * n * n)
        early = call(
            functools.partial(early_kernel, sizes), field, [load, applied, scatter, near[0], near[2]], flops // 2
        )
        resid, coarse = call(
            functools.partial(resid_kernel, sizes),
            [shape((n, cases), BF), vector],
            [early, scatter, based_t, near[1], near[3]],
            flops // 2,
        )
        vectors = {}
        for dr, dc in far_moves:
            got = coarse if dr + dc == 0 else send(coarse, swap_pairs(0, dr, dc))
            vectors[0, dr, dc] = got
            for dg in range(1, grps):
                vectors[dg, dr, dc] = send(got, swap_pairs(dg, 0, 0))
        if sweep:
            fix, *own = call(fix_kernel, [field] + [edge] * 4, [pre_sel, resid], flops)
        else:
            fix, *own = call(fix_plain_kernel, [field] + [edge] * 4, [pre, sel, resid], 2 * flops)
        near = halo(own)
        mine, *others = call(
            functools.partial(coarse_kernel, stepwise, geometry, row_size, nb, moves),
            [shape((nb, cases), F32)] + [vector] * (lines - 1),
            [*blocks, *(vectors[move] for move in moves)],
            2 * lines * nb * 2 * nb * grid_rows * cases,
            [pltpu.VMEM((2 * grid_rows * nb, cases), BF), pltpu.VMEM((lines * nb, cases), F32)],
        )
        others = [send(o, swap_pairs(0, 0, 2 * (k + 1))) for k, o in enumerate(others)]
        if sweep < ITERS - 1:
            if sweep == 0:
                lift = call(product_kernel, thin, [op, based], n * n * nb)
            u, applied = call(
                functools.partial(middle_kernel, sizes), [field] * 2, [op, u, fix, scatter, *near], 2 * flops, scratch
            )
            solved, applied, *edges = call(
                next_kernel, [vector, field] + [edge] * 4, [lift, sel, applied, mine, *others], flops
            )
            near = halo(edges)
        else:
            u = call(
                functools.partial(late_kernel, sizes), field, [u, fix, scatter, based, solved, *near], flops, scratch
            )
            u = call(
                last_kernel,
                field,
                [u, based, mine, *others],
                n * nb * cases,
                [pltpu.VMEM((n, cases), F32), pltpu.SemaphoreType.DMA((CHUNKS,))],
                far_out=True,
            )
    return u[None, None]


def solution(mesh):
    cells = P(("grp", "row"), "col", None, None)
    lists = P(("grp", "row"), "col", None)

    return jax.shard_map(
        body,
        mesh=mesh,
        in_specs=(cells, cells, cells, cells, cells, P(("grp", "row"), "col"), lists, lists),
        out_specs=cells,
        check_vma=False,
    )
```

```python
import functools

import jax
import jax.numpy as jnp
from jax import lax
from jax.experimental import pallas as pl
from jax.experimental.pallas import tpu as pltpu
from jax.sharding import PartitionSpec as P


ITERS = 2
OMEGA = 0.6
AXES = ("grp", "row", "col")
BF = jnp.bfloat16
F32 = jnp.float32
VMEM_LIMIT = 24 << 20
CHUNKS = 4


def dot(a, b):
    return jnp.dot(a, b, preferred_element_type=F32)


def call(kernel, outs, args, flops, scratch=(), far=(), far_out=False):
    moved = sum(a.size * a.dtype.itemsize for a in args)
    vmem, hbm = pl.BlockSpec(memory_space=pltpu.VMEM), pl.BlockSpec(memory_space=pltpu.HBM)
    out_spec = hbm if far_out else vmem
    args = [pltpu.with_memory_space_constraint(a, pltpu.HBM) if k in far else a for k, a in enumerate(args)]
    return pl.pallas_call(
        kernel,
        out_shape=outs,
        in_specs=[hbm if k in far else vmem for k in range(len(args))],
        out_specs=[out_spec] * len(outs) if isinstance(outs, list) else out_spec,
        scratch_shapes=list(scratch),
        compiler_params=pltpu.CompilerParams(vmem_limit_bytes=VMEM_LIMIT),
        cost_estimate=pl.CostEstimate(flops=flops, transcendentals=0, bytes_accessed=moved),
    )(*args)


def chunk_copies(source, target, sems, first, count):
    rows = source.shape[0] // count
    return [
        pltpu.make_async_copy(
            source.at[pl.ds(k * rows, rows)], target.at[pl.ds(k * rows, rows)], sems.at[first + k]
        )
        for k in range(count)
    ]


def shape(dims, dtype):
    return jax.ShapeDtypeStruct(tuple(dims), dtype)


def pairs_of(sizes, where):
    grps, rows, cols = sizes
    flat = lambda g, r, c: (g * rows + r) * cols + c
    return [
        (flat(g, r, c), flat(*where(g, r, c)))
        for g in range(grps)
        for r in range(rows)
        for c in range(cols)
    ]


def matching(sizes, odd, along_cols):
    grps, rows, cols = sizes
    count = cols if along_cols else grps * rows

    def where(g, r, c):
        at = c if along_cols else g * rows + r
        to = at + 1 if at % 2 == odd else at - 1
        if 0 <= to < count:
            return (g, r, to) if along_cols else (to // rows, to % rows, c)
        if along_cols and grps == 2:
            return (1 - g, r, c)
        if not along_cols:
            to = count - 1 - at
            return (to // rows, to % rows, c)
        return (g, r, c)

    return pairs_of(sizes, where)


def send(value, pairs):
    return lax.ppermute(value, AXES, pairs)


def edge_of(sizes, m):
    _, rows, _ = sizes
    if m < 2:
        at, up, down = lax.axis_index("col"), 1, 0
    else:
        at, up, down = lax.axis_index("grp") * rows + lax.axis_index("row"), 3, 2
    return jnp.where(at % 2 == m % 2, up, down)


def edge_list(sizes, lists_ref, m):
    part = lists_ref.shape[1] // 4
    at = pl.multiple_of(edge_of(sizes, m) * part, part)
    return lists_ref[:, pl.ds(at, part)]


def load_kernel(sizes, nb, lists_hbm, op_hbm, u_hbm, *refs):
    if len(refs) > 5:
        inverse_hbm, lists_ref, sel_ref, op_ref, u_ref, keep_ref, give_ref, sems = refs
    else:
        lists_ref, sel_ref, op_ref, u_ref, sems = refs
    named = pltpu.make_async_copy(lists_hbm, lists_ref, sems.at[0])
    copies = []
    if len(refs) > 5:
        parity = lax.axis_index("col") % 2
        lines = keep_ref.shape[0] // nb
        for line in range(lines):
            for k, (ref, mine) in enumerate(((keep_ref, parity), (give_ref, 1 - parity))):
                rows = pl.ds(pl.multiple_of((2 * line + mine) * nb, nb), nb)
                sem = sems.at[1 + 2 * CHUNKS + 2 * line + k]
                copies.append(pltpu.make_async_copy(inverse_hbm.at[rows], ref.at[pl.ds(line * nb, nb)], sem))
    copies += chunk_copies(u_hbm, u_ref, sems, 1, CHUNKS)
    copies += chunk_copies(op_hbm, op_ref, sems, 1 + CHUNKS, CHUNKS)
    for copy in [named] + copies:
        copy.start()
    named.wait()
    n = sel_ref.shape[0]
    part = n // 4
    for m in range(4):
        names = jnp.broadcast_to(edge_list(sizes, lists_ref, m), (128, part)).T
        lanes = lax.broadcasted_iota(jnp.int32, (part, 128), 1)
        for j in range(n // 128):
            hit = names == lanes + j * 128
            sel_ref[m * part : (m + 1) * part, j * 128 : (j + 1) * 128] = jnp.where(hit, 1.0, 0.0).astype(BF)
    for copy in copies:
        copy.wait()


def apply_kernel(op_ref, u_ref, sel_ref, applied_ref, *edges):
    applied = dot(op_ref[...], u_ref[...].astype(BF))
    applied_ref[...] = applied
    split_edges(applied, sel_ref, edges)


def split_edges(field, sel_ref, edges):
    field = field.astype(BF)
    part = edges[0].shape[0]
    for m, edge in enumerate(edges):
        edge[...] = dot(sel_ref[m * part : (m + 1) * part, :], field).astype(BF)


def tables_kernel(sizes, lists_ref, basis_t_ref, slot_ref, scatter_ref, based_ref, based_t_ref):
    n = scatter_ref.shape[0]
    part = n // 4
    for m in range(4):
        rows = lax.broadcasted_iota(jnp.int32, (n, part), 0)
        hit = rows == edge_list(sizes, lists_ref, m)
        scatter_ref[:, m * part : (m + 1) * part] = jnp.where(hit, 1.0, 0.0).astype(BF)
    nb = basis_t_ref.shape[0]
    pick = lax.broadcasted_iota(jnp.int32, (nb, nb), 0) == slot_ref[...]
    based_t = dot(jnp.where(pick, 1.0, 0.0).astype(BF), basis_t_ref[...])
    based_t_ref[...] = based_t.astype(BF)
    based_ref[...] = based_t.T.astype(BF)


def product_kernel(left_ref, right_ref, out_ref):
    out_ref[...] = dot(left_ref[...], right_ref[...]).astype(BF)


def shared(sizes):
    grps, rows, cols = sizes
    a = lax.axis_index("grp") * rows + lax.axis_index("row")
    c = lax.axis_index("col")

    def partner(at, count, odd):
        up = at % 2 == odd
        return jnp.where(up, at + 1 < count, at > 0)

    return [
        partner(c, cols, 0),
        partner(c, cols, 1),
        partner(a, grps * rows, 0),
        partner(a, grps * rows, 1),
    ]


def scattered(sizes, scatter_ref, near, which):
    part = near[0].shape[0]
    there = shared(sizes)
    total = None
    for m, got in zip(which, near):
        got = jnp.where(there[m], got[...], jnp.zeros_like(got))
        add = dot(scatter_ref[:, m * part : (m + 1) * part], got)
        total = add if total is None else total + add
    return total


def early_kernel(sizes, load_ref, applied_ref, scatter_ref, n0, n2, out_ref):
    out_ref[...] = load_ref[...] - applied_ref[...] - scattered(sizes, scatter_ref, (n0, n2), (0, 2))


def resid_kernel(sizes, early_ref, scatter_ref, based_t_ref, n1, n3, resid_ref, coarse_ref):
    resid = (early_ref[...] - scattered(sizes, scatter_ref, (n1, n3), (1, 3))).astype(BF)
    resid_ref[...] = resid
    coarse_ref[...] = dot(based_t_ref[...], resid).astype(BF)


def fix_plain_kernel(pre_ref, sel_ref, resid_ref, fix_ref, *edges):
    fix = dot(pre_ref[...], resid_ref[...]).astype(BF)
    part = edges[0].shape[0]
    for m, edge in enumerate(edges):
        rows = slice(m * part, (m + 1) * part)
        own = dot(sel_ref[rows, :], fix)
        fix_ref[rows, :] = own
        edge[...] = own.astype(BF)


def fix_kernel(pre_sel_ref, resid_ref, fix_ref, *edges):
    part = edges[0].shape[0]
    for m, edge in enumerate(edges):
        rows = slice(m * part, (m + 1) * part)
        fix = dot(pre_sel_ref[rows, :], resid_ref[...])
        fix_ref[rows, :] = fix
        edge[...] = fix.astype(BF)


def smoothed(sizes, u, fix_ref, scatter_ref, near, which):
    part = near[0].shape[0]
    there = shared(sizes)
    total = None
    for m, got in zip(which, near):
        rows = slice(m * part, (m + 1) * part)
        fix = fix_ref[rows, :]
        both = jnp.where(there[m], 0.5 * (fix + got[...].astype(F32)), fix).astype(BF)
        add = dot(scatter_ref[:, rows], both)
        total = add if total is None else total + add
    return u + OMEGA * total


def first_kernel(sizes, u_ref, fix_ref, scatter_ref, n0, n2, out_ref):
    out_ref[...] = smoothed(sizes, u_ref[...], fix_ref, scatter_ref, (n0, n2), (0, 2))


def middle_kernel(sizes, op_ref, u_ref, fix_ref, scatter_ref, n1, n3, out_ref, applied_ref):
    u = smoothed(sizes, u_ref[...], fix_ref, scatter_ref, (n1, n3), (1, 3))
    out_ref[...] = u
    applied_ref[...] = dot(op_ref[...], u.astype(BF))


def solution_of(mine_ref, others):
    solved = mine_ref[...]
    for other in others:
        solved = solved + other[...].astype(F32)
    return solved.astype(BF)


def next_kernel(lift_ref, sel_ref, applied_ref, mine_ref, *refs):
    others, (solved_ref, out_ref, *edges) = refs[:-6], refs[-6:]
    solved = solution_of(mine_ref, others)
    solved_ref[...] = solved
    applied = applied_ref[...] + OMEGA * dot(lift_ref[...], solved)
    out_ref[...] = applied
    split_edges(applied, sel_ref, edges)


def late_kernel(sizes, u_ref, fix_ref, scatter_ref, based_ref, solved_ref, n1, n3, out_ref):
    u = u_ref[...] + OMEGA * dot(based_ref[...], solved_ref[...])
    out_ref[...] = smoothed(sizes, u, fix_ref, scatter_ref, (n1, n3), (1, 3))


def last_kernel(u_ref, based_ref, mine_ref, *refs):
    others, (out_hbm, total, sems) = refs[:-3], refs[-3:]
    solved = solution_of(mine_ref, others)
    copies = chunk_copies(total, out_hbm, sems, 0, CHUNKS)
    rows = total.shape[0] // CHUNKS
    for k, copy in enumerate(copies):
        at = slice(k * rows, (k + 1) * rows)
        total[at, :] = u_ref[at, :] + OMEGA * dot(based_ref[at, :], solved)
        copy.start()
    for copy in copies:
        copy.wait()


def regroup_kernel(geometry, nb, inverse_ref, *blocks):
    _, ratio, lines = geometry
    c = lax.axis_index("col")
    owner = c // ratio
    for k, block in enumerate(blocks):
        target = k ^ owner
        parity, pair = target % 2, target // 2
        for line in range(lines):
            rows = pl.ds(pl.multiple_of((2 * line + parity) * nb, nb), nb)
            cols = pl.ds(pl.multiple_of(pair * 2 * nb, 2 * nb), 2 * nb)
            block[line * nb : (line + 1) * nb, :] = inverse_ref[rows, cols]


def upper_kernel(top, mine_ref, got_ref, keep_ref, give_ref):
    c = lax.axis_index("col")
    same = c % 2 == c // top
    keep_ref[...] = jnp.where(same, mine_ref[...], got_ref[...])
    give_ref[...] = jnp.where(same, got_ref[...], mine_ref[...])


def lower_kernel(first_ref, second_ref, keep_ref, give_ref):
    low = (lax.axis_index("col") // 2) % 2
    half = first_ref.shape[1] // 2
    for k, source in enumerate((first_ref, second_ref)):
        left, right = source[:, :half], source[:, half:]
        keep_ref[:, k * half : (k + 1) * half] = jnp.where(low == 0, left, right)
        give_ref[:, k * half : (k + 1) * half] = jnp.where(low == 0, right, left)


def coarse_kernel(stepwise, geometry, row_size, nb, moves, *refs):
    grid_rows, _, lines = geometry
    width = 2 * nb
    count = 2 if stepwise else grid_rows
    arrays, refs = refs[:count], refs[count:]
    vectors, refs = refs[: len(moves)], refs[len(moves) :]
    mine_ref, others, (stack, total) = refs[0], refs[1:lines], refs[lines:]
    g, r, c = (lax.axis_index(axis) for axis in AXES)
    line = c // 2
    for (dg, dr, dc), vector in zip(moves, vectors):
        at = (((g ^ dg) * row_size + (r ^ dr)) * 2 + ((c % 2) ^ dc)) * nb
        stack[pl.ds(pl.multiple_of(at, nb), nb), :] = vector[...]
    if stepwise:
        blocks = [
            (arrays[k // 2][:, (k % 2) * width : (k % 2 + 1) * width], line ^ (2 * (k % 2) + k // 2)) for k in range(4)
        ]
    else:
        blocks = [(array[...], k ^ (c % grid_rows)) for k, array in enumerate(arrays)]
    acc = None
    for block, owner in blocks:
        part = dot(block, stack[pl.ds(pl.multiple_of(owner * width, width), width), :])
        acc = part if acc is None else acc + part
    total[...] = acc
    for k in range(lines):
        got = total[pl.ds(pl.multiple_of((line ^ k) * nb, nb), nb), :]
        if k == 0:
            mine_ref[...] = got
        else:
            others[k - 1][...] = got.astype(BF)


def in_steps(sizes):
    grps, row_size, cols = sizes
    return grps * row_size == 4 and cols == 2 * grps * row_size


def body(load, guess, interface_op, precond, basis, coarse_inverse, edge_rows, coarse_slot):
    sizes = tuple(lax.axis_size(axis) for axis in AXES)
    grps, row_size, cols = sizes
    grid_rows = grps * row_size
    load, u, op, pre = load[0, 0], guess[0, 0], interface_op[0, 0], precond[0, 0]
    basis_t = jnp.swapaxes(basis[0, 0], 0, 1)
    slot, lists = coarse_slot[0], edge_rows[0]
    n, cases = load.shape
    nb = basis_t.shape[0]
    part = n // 4
    ratio, lines = cols // grid_rows, cols // 2
    geometry = (grid_rows, ratio, lines)

    halo_pairs = [matching(sizes, m % 2, m < 2) for m in range(4)]
    far_moves = [(dr, dc) for dr in range(row_size) for dc in range(2)]
    moves = [(dg, dr, dc) for dr, dc in far_moves for dg in range(grps)]

    def swap_pairs(dg, dr, dc):
        return pairs_of(sizes, lambda g, r, c: (g ^ dg, r ^ dr, c ^ dc))

    def target(k):
        return pairs_of(sizes, lambda g, r, c: (g, r, (c % ratio) * grid_rows + (k ^ (c // ratio))))

    field = shape((n, cases), F32)
    edge = shape((part, cases), BF)
    square = shape((n, n), BF)
    thin = shape((n, nb), BF)
    vector = shape((nb, cases), BF)
    flops = 2 * n * n * cases

    def halo(edges):
        return [send(e, p) for e, p in zip(edges, halo_pairs)]

    stepwise = in_steps(sizes)
    half = shape((lines * nb, coarse_inverse.shape[1]), BF)
    lists, sel, op, u, *halves = call(
        functools.partial(load_kernel, sizes, nb),
        [shape(lists.shape, lists.dtype), square, square, field] + [half, half] * stepwise,
        [lists, op, u] + [coarse_inverse] * stepwise,
        n * n,
        [pltpu.SemaphoreType.DMA((1 + 2 * CHUNKS + 2 * lines,))],
        far=(0, 1, 2, 3),
    )
    if stepwise:
        keep, give = halves
        got = send(give, swap_pairs(0, 0, 1))
    else:
        blocks = call(
            functools.partial(regroup_kernel, geometry, nb),
            [shape((lines * nb, 2 * nb), BF)] * grid_rows,
            [coarse_inverse],
            n,
        )
        blocks = [send(block, target(k)) for k, block in enumerate(blocks)]
    applied, *edges = call(apply_kernel, [field] + [edge] * 4, [op, u, sel], 2 * flops)
    near = halo(edges)
    if stepwise:
        keep, give = call(functools.partial(upper_kernel, cols // 2), [half, half], [keep, got], n)
        got = send(give, swap_pairs(0, 0, cols // 2))
    scatter, based, based_t = call(
        functools.partial(tables_kernel, sizes), [square, thin, shape((nb, n), BF)], [lists, basis_t, slot], n * n
    )
    if stepwise:
        keep, give = call(lower_kernel, [half, half], [keep, got], n)
        blocks = [keep, send(give, swap_pairs(0, 0, 2))]
    for sweep in range(ITERS):
        if sweep == 1:
            pre_sel = call(product_kernel, square, [sel, pre], 2 * n * n * n)
        early = call(
            functools.partial(early_kernel, sizes), field, [load, applied, scatter, near[0], near[2]], flops // 2
        )
        resid, coarse = call(
            functools.partial(resid_kernel, sizes),
            [shape((n, cases), BF), vector],
            [early, scatter, based_t, near[1], near[3]],
            flops // 2,
        )
        vectors = {}
        for dr, dc in far_moves:
            got = coarse if dr + dc == 0 else send(coarse, swap_pairs(0, dr, dc))
            vectors[0, dr, dc] = got
            for dg in range(1, grps):
                vectors[dg, dr, dc] = send(got, swap_pairs(dg, 0, 0))
        if sweep:
            fix, *own = call(fix_kernel, [field] + [edge] * 4, [pre_sel, resid], flops)
        else:
            fix, *own = call(fix_plain_kernel, [field] + [edge] * 4, [pre, sel, resid], 2 * flops)
        near = halo(own)
        mine, *others = call(
            functools.partial(coarse_kernel, stepwise, geometry, row_size, nb, moves),
            [shape((nb, cases), F32)] + [vector] * (lines - 1),
            [*blocks, *(vectors[move] for move in moves)],
            2 * lines * nb * 2 * nb * grid_rows * cases,
            [pltpu.VMEM((2 * grid_rows * nb, cases), BF), pltpu.VMEM((lines * nb, cases), F32)],
        )
        others = [send(o, swap_pairs(0, 0, 2 * (k + 1))) for k, o in enumerate(others)]
        u = call(functools.partial(first_kernel, sizes), field, [u, fix, scatter, near[0], near[2]], flops // 2)
        if sweep < ITERS - 1:
            if sweep == 0:
                lift = call(product_kernel, thin, [op, based], n * n * nb)
            u, applied = call(
                functools.partial(middle_kernel, sizes), [field] * 2, [op, u, fix, scatter, near[1], near[3]], 2 * flops
            )
            solved, applied, *edges = call(
                next_kernel, [vector, field] + [edge] * 4, [lift, sel, applied, mine, *others], flops
            )
            near = halo(edges)
        else:
            u = call(
                functools.partial(late_kernel, sizes),
                field,
                [u, fix, scatter, based, solved, near[1], near[3]],
                flops // 2,
            )
            u = call(
                last_kernel,
                field,
                [u, based, mine, *others],
                n * nb * cases,
                [pltpu.VMEM((n, cases), F32), pltpu.SemaphoreType.DMA((CHUNKS,))],
                far_out=True,
            )
    return u[None, None]


def solution(mesh):
    cells = P(("grp", "row"), "col", None, None)
    lists = P(("grp", "row"), "col", None)

    return jax.shard_map(
        body,
        mesh=mesh,
        in_specs=(cells, cells, cells, cells, cells, P(("grp", "row"), "col"), lists, lists),
        out_specs=cells,
        check_vma=False,
    )
```

```python
import functools

import jax
import jax.numpy as jnp
from jax import lax
from jax.experimental import pallas as pl
from jax.experimental.pallas import tpu as pltpu
from jax.sharding import PartitionSpec as P


ITERS = 2
OMEGA = 0.6
AXES = ("grp", "row", "col")
BF = jnp.bfloat16
F32 = jnp.float32
VMEM_LIMIT = 24 << 20
CHUNKS = 4


def dot(a, b):
    return jnp.dot(a, b, preferred_element_type=F32)


def call(kernel, outs, args, flops, scratch=(), far=(), far_out=False):
    moved = sum(a.size * a.dtype.itemsize for a in args)
    vmem, hbm = pl.BlockSpec(memory_space=pltpu.VMEM), pl.BlockSpec(memory_space=pltpu.HBM)
    out_spec = hbm if far_out else vmem
    args = [pltpu.with_memory_space_constraint(a, pltpu.HBM) if k in far else a for k, a in enumerate(args)]
    return pl.pallas_call(
        kernel,
        out_shape=outs,
        in_specs=[hbm if k in far else vmem for k in range(len(args))],
        out_specs=[out_spec] * len(outs) if isinstance(outs, list) else out_spec,
        scratch_shapes=list(scratch),
        compiler_params=pltpu.CompilerParams(vmem_limit_bytes=VMEM_LIMIT),
        cost_estimate=pl.CostEstimate(flops=flops, transcendentals=0, bytes_accessed=moved),
    )(*args)


def chunk_copies(source, target, sems, first, count):
    rows = source.shape[0] // count
    return [
        pltpu.make_async_copy(
            source.at[pl.ds(k * rows, rows)], target.at[pl.ds(k * rows, rows)], sems.at[first + k]
        )
        for k in range(count)
    ]


def shape(dims, dtype):
    return jax.ShapeDtypeStruct(tuple(dims), dtype)


def pairs_of(sizes, where):
    grps, rows, cols = sizes
    flat = lambda g, r, c: (g * rows + r) * cols + c
    return [
        (flat(g, r, c), flat(*where(g, r, c)))
        for g in range(grps)
        for r in range(rows)
        for c in range(cols)
    ]


def matching(sizes, odd, along_cols):
    grps, rows, cols = sizes
    count = cols if along_cols else grps * rows

    def where(g, r, c):
        at = c if along_cols else g * rows + r
        to = at + 1 if at % 2 == odd else at - 1
        if 0 <= to < count:
            return (g, r, to) if along_cols else (to // rows, to % rows, c)
        if along_cols and grps == 2:
            return (1 - g, r, c)
        if not along_cols:
            to = count - 1 - at
            return (to // rows, to % rows, c)
        return (g, r, c)

    return pairs_of(sizes, where)


def send(value, pairs):
    return lax.ppermute(value, AXES, pairs)


def edge_of(sizes, m):
    _, rows, _ = sizes
    if m < 2:
        at, up, down = lax.axis_index("col"), 1, 0
    else:
        at, up, down = lax.axis_index("grp") * rows + lax.axis_index("row"), 3, 2
    return jnp.where(at % 2 == m % 2, up, down)


def edge_list(sizes, lists_ref, m):
    part = lists_ref.shape[1] // 4
    at = pl.multiple_of(edge_of(sizes, m) * part, part)
    return lists_ref[:, pl.ds(at, part)]


def load_kernel(sizes, nb, lists_hbm, op_hbm, u_hbm, *refs):
    if len(refs) > 5:
        inverse_hbm, lists_ref, sel_ref, op_ref, u_ref, keep_ref, give_ref, sems = refs
    else:
        lists_ref, sel_ref, op_ref, u_ref, sems = refs
    named = pltpu.make_async_copy(lists_hbm, lists_ref, sems.at[0])
    copies = []
    if len(refs) > 5:
        parity = lax.axis_index("col") % 2
        lines = keep_ref.shape[0] // nb
        for line in range(lines):
            for k, (ref, mine) in enumerate(((keep_ref, parity), (give_ref, 1 - parity))):
                rows = pl.ds(pl.multiple_of((2 * line + mine) * nb, nb), nb)
                sem = sems.at[1 + 2 * CHUNKS + 2 * line + k]
                copies.append(pltpu.make_async_copy(inverse_hbm.at[rows], ref.at[pl.ds(line * nb, nb)], sem))
    copies += chunk_copies(u_hbm, u_ref, sems, 1, CHUNKS)
    copies += chunk_copies(op_hbm, op_ref, sems, 1 + CHUNKS, CHUNKS)
    for copy in [named] + copies:
        copy.start()
    named.wait()
    n = sel_ref.shape[0]
    part = n // 4
    for m in range(4):
        names = jnp.broadcast_to(edge_list(sizes, lists_ref, m), (128, part)).T
        lanes = lax.broadcasted_iota(jnp.int32, (part, 128), 1)
        for j in range(n // 128):
            hit = names == lanes + j * 128
            sel_ref[m * part : (m + 1) * part, j * 128 : (j + 1) * 128] = jnp.where(hit, 1.0, 0.0).astype(BF)
    for copy in copies:
        copy.wait()


def apply_kernel(op_ref, u_ref, sel_ref, applied_ref, *edges):
    applied = dot(op_ref[...], u_ref[...].astype(BF))
    applied_ref[...] = applied
    split_edges(applied, sel_ref, edges)


def split_edges(field, sel_ref, edges):
    field = field.astype(BF)
    part = edges[0].shape[0]
    for m, edge in enumerate(edges):
        edge[...] = dot(sel_ref[m * part : (m + 1) * part, :], field).astype(BF)


def tables_kernel(sizes, lists_ref, basis_t_ref, slot_ref, scatter_ref, based_ref, based_t_ref):
    n = scatter_ref.shape[0]
    part = n // 4
    for m in range(4):
        rows = lax.broadcasted_iota(jnp.int32, (n, part), 0)
        hit = rows == edge_list(sizes, lists_ref, m)
        scatter_ref[:, m * part : (m + 1) * part] = jnp.where(hit, 1.0, 0.0).astype(BF)
    nb = basis_t_ref.shape[0]
    pick = lax.broadcasted_iota(jnp.int32, (nb, nb), 0) == slot_ref[...]
    based_t = dot(jnp.where(pick, 1.0, 0.0).astype(BF), basis_t_ref[...])
    based_t_ref[...] = based_t.astype(BF)
    based_ref[...] = based_t.T.astype(BF)


def product_kernel(left_ref, right_ref, out_ref):
    out_ref[...] = dot(left_ref[...], right_ref[...]).astype(BF)


def shared(sizes):
    grps, rows, cols = sizes
    a = lax.axis_index("grp") * rows + lax.axis_index("row")
    c = lax.axis_index("col")

    def partner(at, count, odd):
        up = at % 2 == odd
        return jnp.where(up, at + 1 < count, at > 0)

    return [
        partner(c, cols, 0),
        partner(c, cols, 1),
        partner(a, grps * rows, 0),
        partner(a, grps * rows, 1),
    ]


def scattered(sizes, scatter_ref, near, which):
    part = near[0].shape[0]
    there = shared(sizes)
    total = None
    for m, got in zip(which, near):
        got = jnp.where(there[m], got[...], jnp.zeros_like(got))
        add = dot(scatter_ref[:, m * part : (m + 1) * part], got)
        total = add if total is None else total + add
    return total


def early_kernel(sizes, load_ref, applied_ref, scatter_ref, n0, n2, out_ref):
    out_ref[...] = load_ref[...] - applied_ref[...] - scattered(sizes, scatter_ref, (n0, n2), (0, 2))


def resid_kernel(sizes, early_ref, scatter_ref, based_t_ref, n1, n3, resid_ref, coarse_ref):
    resid = (early_ref[...] - scattered(sizes, scatter_ref, (n1, n3), (1, 3))).astype(BF)
    resid_ref[...] = resid
    coarse_ref[...] = dot(based_t_ref[...], resid).astype(BF)


def fix_plain_kernel(pre_ref, sel_ref, resid_ref, fix_ref, *edges):
    fix = dot(pre_ref[...], resid_ref[...]).astype(BF)
    part = edges[0].shape[0]
    for m, edge in enumerate(edges):
        rows = slice(m * part, (m + 1) * part)
        own = dot(sel_ref[rows, :], fix)
        fix_ref[rows, :] = own
        edge[...] = own.astype(BF)


def fix_kernel(pre_sel_ref, resid_ref, fix_ref, *edges):
    part = edges[0].shape[0]
    for m, edge in enumerate(edges):
        rows = slice(m * part, (m + 1) * part)
        fix = dot(pre_sel_ref[rows, :], resid_ref[...])
        fix_ref[rows, :] = fix
        edge[...] = fix.astype(BF)


def smoothed(sizes, u, fix_ref, scatter_ref, near, which):
    part = near[0].shape[0]
    there = shared(sizes)
    total = None
    for m, got in zip(which, near):
        rows = slice(m * part, (m + 1) * part)
        fix = fix_ref[rows, :]
        both = jnp.where(there[m], 0.5 * (fix + got[...].astype(F32)), fix).astype(BF)
        add = dot(scatter_ref[:, rows], both)
        total = add if total is None else total + add
    return u + OMEGA * total


def first_kernel(sizes, u_ref, fix_ref, scatter_ref, n0, n2, out_ref):
    out_ref[...] = smoothed(sizes, u_ref[...], fix_ref, scatter_ref, (n0, n2), (0, 2))


def middle_kernel(sizes, op_ref, u_ref, fix_ref, scatter_ref, n1, n3, out_ref, applied_ref):
    u = smoothed(sizes, u_ref[...], fix_ref, scatter_ref, (n1, n3), (1, 3))
    out_ref[...] = u
    applied_ref[...] = dot(op_ref[...], u.astype(BF))


def solution_of(mine_ref, others):
    solved = mine_ref[...]
    for other in others:
        solved = solved + other[...].astype(F32)
    return solved.astype(BF)


def next_kernel(lift_ref, sel_ref, applied_ref, mine_ref, *refs):
    others, (solved_ref, out_ref, *edges) = refs[:-6], refs[-6:]
    solved = solution_of(mine_ref, others)
    solved_ref[...] = solved
    applied = applied_ref[...] + OMEGA * dot(lift_ref[...], solved)
    out_ref[...] = applied
    split_edges(applied, sel_ref, edges)


def late_kernel(sizes, u_ref, fix_ref, scatter_ref, based_ref, solved_ref, n1, n3, out_ref):
    u = u_ref[...] + OMEGA * dot(based_ref[...], solved_ref[...])
    out_ref[...] = smoothed(sizes, u, fix_ref, scatter_ref, (n1, n3), (1, 3))


def last_kernel(u_ref, based_ref, mine_ref, *refs):
    others, (out_hbm, total, sems) = refs[:-3], refs[-3:]
    solved = solution_of(mine_ref, others)
    copies = chunk_copies(total, out_hbm, sems, 0, CHUNKS)
    rows = total.shape[0] // CHUNKS
    for k, copy in enumerate(copies):
        at = slice(k * rows, (k + 1) * rows)
        total[at, :] = u_ref[at, :] + OMEGA * dot(based_ref[at, :], solved)
        copy.start()
    for copy in copies:
        copy.wait()


def regroup_kernel(geometry, nb, inverse_ref, *blocks):
    _, ratio, lines = geometry
    c = lax.axis_index("col")
    owner = c // ratio
    for k, block in enumerate(blocks):
        target = k ^ owner
        parity, pair = target % 2, target // 2
        for line in range(lines):
            rows = pl.ds(pl.multiple_of((2 * line + parity) * nb, nb), nb)
            cols = pl.ds(pl.multiple_of(pair * 2 * nb, 2 * nb), 2 * nb)
            block[line * nb : (line + 1) * nb, :] = inverse_ref[rows, cols]


def upper_kernel(top, mine_ref, got_ref, keep_ref, give_ref):
    c = lax.axis_index("col")
    same = c % 2 == c // top
    keep_ref[...] = jnp.where(same, mine_ref[...], got_ref[...])
    give_ref[...] = jnp.where(same, got_ref[...], mine_ref[...])


def lower_kernel(first_ref, second_ref, keep_ref, give_ref):
    low = (lax.axis_index("col") // 2) % 2
    half = first_ref.shape[1] // 2
    for k, source in enumerate((first_ref, second_ref)):
        left, right = source[:, :half], source[:, half:]
        keep_ref[:, k * half : (k + 1) * half] = jnp.where(low == 0, left, right)
        give_ref[:, k * half : (k + 1) * half] = jnp.where(low == 0, right, left)


def pair_kernel(mine_ref, *refs):
    others, out_ref = refs[:-1], refs[-1]
    nb = mine_ref.shape[0]
    g = lax.axis_index("grp")
    for dg, ref in enumerate((mine_ref, *others)):
        out_ref[pl.ds(pl.multiple_of((g ^ dg) * nb, nb), nb), :] = ref[...]


def coarse_kernel(stepwise, geometry, row_size, nb, moves, *refs):
    grid_rows, _, lines = geometry
    width = 2 * nb
    count = 2 if stepwise else grid_rows
    arrays, refs = refs[:count], refs[count:]
    vectors, refs = refs[: len(moves)], refs[len(moves) :]
    mine_ref, others, (stack, total) = refs[0], refs[1:lines], refs[lines:]
    r, c = lax.axis_index("row"), lax.axis_index("col")
    line = c // 2
    for (dr, dc), vector in zip(moves, vectors):
        for core in range(vector.shape[0] // nb):
            at = ((core * row_size + (r ^ dr)) * 2 + ((c % 2) ^ dc)) * nb
            stack[pl.ds(pl.multiple_of(at, nb), nb), :] = vector[core * nb : (core + 1) * nb, :]
    if stepwise:
        blocks = [
            (arrays[k // 2][:, (k % 2) * width : (k % 2 + 1) * width], line ^ (2 * (k % 2) + k // 2)) for k in range(4)
        ]
    else:
        blocks = [(array[...], k ^ (c % grid_rows)) for k, array in enumerate(arrays)]
    acc = None
    for block, owner in blocks:
        part = dot(block, stack[pl.ds(pl.multiple_of(owner * width, width), width), :])
        acc = part if acc is None else acc + part
    total[...] = acc
    for k in range(lines):
        got = total[pl.ds(pl.multiple_of((line ^ k) * nb, nb), nb), :]
        if k == 0:
            mine_ref[...] = got
        else:
            others[k - 1][...] = got.astype(BF)


def in_steps(sizes):
    grps, row_size, cols = sizes
    return grps * row_size == 4 and cols == 2 * grps * row_size


def body(load, guess, interface_op, precond, basis, coarse_inverse, edge_rows, coarse_slot):
    sizes = tuple(lax.axis_size(axis) for axis in AXES)
    grps, row_size, cols = sizes
    grid_rows = grps * row_size
    load, u, op, pre = load[0, 0], guess[0, 0], interface_op[0, 0], precond[0, 0]
    basis_t = jnp.swapaxes(basis[0, 0], 0, 1)
    slot, lists = coarse_slot[0], edge_rows[0]
    n, cases = load.shape
    nb = basis_t.shape[0]
    part = n // 4
    ratio, lines = cols // grid_rows, cols // 2
    geometry = (grid_rows, ratio, lines)

    halo_pairs = [matching(sizes, m % 2, m < 2) for m in range(4)]
    far_moves = [(dr, dc) for dr in range(row_size) for dc in range(2)]

    def swap_pairs(dg, dr, dc):
        return pairs_of(sizes, lambda g, r, c: (g ^ dg, r ^ dr, c ^ dc))

    def target(k):
        return pairs_of(sizes, lambda g, r, c: (g, r, (c % ratio) * grid_rows + (k ^ (c // ratio))))

    field = shape((n, cases), F32)
    edge = shape((part, cases), BF)
    square = shape((n, n), BF)
    thin = shape((n, nb), BF)
    vector = shape((nb, cases), BF)
    flops = 2 * n * n * cases

    def halo(edges):
        return [send(e, p) for e, p in zip(edges, halo_pairs)]

    stepwise = in_steps(sizes)
    half = shape((lines * nb, coarse_inverse.shape[1]), BF)
    lists, sel, op, u, *halves = call(
        functools.partial(load_kernel, sizes, nb),
        [shape(lists.shape, lists.dtype), square, square, field] + [half, half] * stepwise,
        [lists, op, u] + [coarse_inverse] * stepwise,
        n * n,
        [pltpu.SemaphoreType.DMA((1 + 2 * CHUNKS + 2 * lines,))],
        far=(0, 1, 2, 3),
    )
    if stepwise:
        keep, give = halves
        got = send(give, swap_pairs(0, 0, 1))
    else:
        blocks = call(
            functools.partial(regroup_kernel, geometry, nb),
            [shape((lines * nb, 2 * nb), BF)] * grid_rows,
            [coarse_inverse],
            n,
        )
        blocks = [send(block, target(k)) for k, block in enumerate(blocks)]
    applied, *edges = call(apply_kernel, [field] + [edge] * 4, [op, u, sel], 2 * flops)
    near = halo(edges)
    if stepwise:
        keep, give = call(functools.partial(upper_kernel, cols // 2), [half, half], [keep, got], n)
        got = send(give, swap_pairs(0, 0, cols // 2))
    scatter, based, based_t = call(
        functools.partial(tables_kernel, sizes), [square, thin, shape((nb, n), BF)], [lists, basis_t, slot], n * n
    )
    if stepwise:
        keep, give = call(lower_kernel, [half, half], [keep, got], n)
        blocks = [keep, send(give, swap_pairs(0, 0, 2))]
    for sweep in range(ITERS):
        if sweep == 1:
            pre_sel = call(product_kernel, square, [sel, pre], 2 * n * n * n)
        early = call(
            functools.partial(early_kernel, sizes), field, [load, applied, scatter, near[0], near[2]], flops // 2
        )
        resid, coarse = call(
            functools.partial(resid_kernel, sizes),
            [shape((n, cases), BF), vector],
            [early, scatter, based_t, near[1], near[3]],
            flops // 2,
        )
        cores = [coarse] + [send(coarse, swap_pairs(dg, 0, 0)) for dg in range(1, grps)]
        pair = call(pair_kernel, shape((grps * nb, cases), BF), cores, n)
        vectors = [send(pair, swap_pairs(0, dr, dc)) if dr + dc else pair for dr, dc in far_moves]
        if sweep:
            fix, *own = call(fix_kernel, [field] + [edge] * 4, [pre_sel, resid], flops)
        else:
            fix, *own = call(fix_plain_kernel, [field] + [edge] * 4, [pre, sel, resid], 2 * flops)
        near = halo(own)
        mine, *others = call(
            functools.partial(coarse_kernel, stepwise, geometry, row_size, nb, far_moves),
            [shape((nb, cases), F32)] + [vector] * (lines - 1),
            [*blocks, *vectors],
            2 * lines * nb * 2 * nb * grid_rows * cases,
            [pltpu.VMEM((2 * grid_rows * nb, cases), BF), pltpu.VMEM((lines * nb, cases), F32)],
        )
        others = [send(o, swap_pairs(0, 0, 2 * (k + 1))) for k, o in enumerate(others)]
        u = call(functools.partial(first_kernel, sizes), field, [u, fix, scatter, near[0], near[2]], flops // 2)
        if sweep < ITERS - 1:
            if sweep == 0:
                lift = call(product_kernel, thin, [op, based], n * n * nb)
            u, applied = call(
                functools.partial(middle_kernel, sizes), [field] * 2, [op, u, fix, scatter, near[1], near[3]], 2 * flops
            )
            solved, applied, *edges = call(
                next_kernel, [vector, field] + [edge] * 4, [lift, sel, applied, mine, *others], flops
            )
            near = halo(edges)
        else:
            u = call(
                functools.partial(late_kernel, sizes),
                field,
                [u, fix, scatter, based, solved, near[1], near[3]],
                flops // 2,
            )
            u = call(
                last_kernel,
                field,
                [u, based, mine, *others],
                n * nb * cases,
                [pltpu.VMEM((n, cases), F32), pltpu.SemaphoreType.DMA((CHUNKS,))],
                far_out=True,
            )
    return u[None, None]


def solution(mesh):
    cells = P(("grp", "row"), "col", None, None)
    lists = P(("grp", "row"), "col", None)

    return jax.shard_map(
        body,
        mesh=mesh,
        in_specs=(cells, cells, cells, cells, cells, P(("grp", "row"), "col"), lists, lists),
        out_specs=cells,
        check_vma=False,
    )
```

```python
import functools

import jax
import jax.numpy as jnp
from jax import lax
from jax.experimental import pallas as pl
from jax.experimental.pallas import tpu as pltpu
from jax.sharding import PartitionSpec as P


ITERS = 2
OMEGA = 0.6
AXES = ("grp", "row", "col")
BF = jnp.bfloat16
F32 = jnp.float32
VMEM_LIMIT = 24 << 20
CHUNKS = 4


def dot(a, b):
    return jnp.dot(a, b, preferred_element_type=F32)


def call(kernel, outs, args, flops, scratch=(), far=(), far_out=False):
    moved = sum(a.size * a.dtype.itemsize for a in args)
    vmem, hbm = pl.BlockSpec(memory_space=pltpu.VMEM), pl.BlockSpec(memory_space=pltpu.HBM)
    out_spec = hbm if far_out else vmem
    args = [pltpu.with_memory_space_constraint(a, pltpu.HBM) if k in far else a for k, a in enumerate(args)]
    return pl.pallas_call(
        kernel,
        out_shape=outs,
        in_specs=[hbm if k in far else vmem for k in range(len(args))],
        out_specs=[out_spec] * len(outs) if isinstance(outs, list) else out_spec,
        scratch_shapes=list(scratch),
        compiler_params=pltpu.CompilerParams(vmem_limit_bytes=VMEM_LIMIT),
        cost_estimate=pl.CostEstimate(flops=flops, transcendentals=0, bytes_accessed=moved),
    )(*args)


def chunk_copies(source, target, sems, first, count):
    rows = source.shape[0] // count
    return [
        pltpu.make_async_copy(
            source.at[pl.ds(k * rows, rows)], target.at[pl.ds(k * rows, rows)], sems.at[first + k]
        )
        for k in range(count)
    ]


def shape(dims, dtype):
    return jax.ShapeDtypeStruct(tuple(dims), dtype)


def pairs_of(sizes, where):
    grps, rows, cols = sizes
    flat = lambda g, r, c: (g * rows + r) * cols + c
    return [
        (flat(g, r, c), flat(*where(g, r, c)))
        for g in range(grps)
        for r in range(rows)
        for c in range(cols)
    ]


def matching(sizes, odd, along_cols):
    grps, rows, cols = sizes
    count = cols if along_cols else grps * rows

    def where(g, r, c):
        at = c if along_cols else g * rows + r
        to = at + 1 if at % 2 == odd else at - 1
        if 0 <= to < count:
            return (g, r, to) if along_cols else (to // rows, to % rows, c)
        if along_cols and grps == 2:
            return (1 - g, r, c)
        if not along_cols:
            to = count - 1 - at
            return (to // rows, to % rows, c)
        return (g, r, c)

    return pairs_of(sizes, where)


def send(value, pairs):
    return lax.ppermute(value, AXES, pairs)


def edge_of(sizes, m):
    _, rows, _ = sizes
    if m < 2:
        at, up, down = lax.axis_index("col"), 1, 0
    else:
        at, up, down = lax.axis_index("grp") * rows + lax.axis_index("row"), 3, 2
    return jnp.where(at % 2 == m % 2, up, down)


def edge_list(sizes, lists_ref, m):
    part = lists_ref.shape[1] // 4
    at = pl.multiple_of(edge_of(sizes, m) * part, part)
    return lists_ref[:, pl.ds(at, part)]


def load_kernel(sizes, nb, lists_hbm, op_hbm, u_hbm, *refs):
    if len(refs) > 5:
        inverse_hbm, lists_ref, sel_ref, op_ref, u_ref, keep_ref, give_ref, sems = refs
    else:
        lists_ref, sel_ref, op_ref, u_ref, sems = refs
    named = pltpu.make_async_copy(lists_hbm, lists_ref, sems.at[0])
    copies = []
    if len(refs) > 5:
        parity = lax.axis_index("col") % 2
        lines = keep_ref.shape[0] // nb
        for line in range(lines):
            for k, (ref, mine) in enumerate(((keep_ref, parity), (give_ref, 1 - parity))):
                rows = pl.ds(pl.multiple_of((2 * line + mine) * nb, nb), nb)
                sem = sems.at[1 + 2 * CHUNKS + 2 * line + k]
                copies.append(pltpu.make_async_copy(inverse_hbm.at[rows], ref.at[pl.ds(line * nb, nb)], sem))
    copies += chunk_copies(u_hbm, u_ref, sems, 1, CHUNKS)
    copies += chunk_copies(op_hbm, op_ref, sems, 1 + CHUNKS, CHUNKS)
    for copy in [named] + copies:
        copy.start()
    named.wait()
    n = sel_ref.shape[0]
    part = n // 4
    for m in range(4):
        names = jnp.broadcast_to(edge_list(sizes, lists_ref, m), (128, part)).T
        lanes = lax.broadcasted_iota(jnp.int32, (part, 128), 1)
        for j in range(n // 128):
            hit = names == lanes + j * 128
            sel_ref[m * part : (m + 1) * part, j * 128 : (j + 1) * 128] = jnp.where(hit, 1.0, 0.0).astype(BF)
    for copy in copies:
        copy.wait()


def apply_kernel(op_ref, u_ref, sel_ref, applied_ref, *edges):
    applied = dot(op_ref[...], u_ref[...].astype(BF))
    applied_ref[...] = applied
    split_edges(applied, sel_ref, edges)


def split_edges(field, sel_ref, edges):
    field = field.astype(BF)
    part = edges[0].shape[0]
    for m, edge in enumerate(edges):
        edge[...] = dot(sel_ref[m * part : (m + 1) * part, :], field).astype(BF)


def tables_kernel(sizes, lists_ref, basis_t_ref, slot_ref, scatter_ref, based_ref, based_t_ref):
    n = scatter_ref.shape[0]
    part = n // 4
    for m in range(4):
        rows = lax.broadcasted_iota(jnp.int32, (n, part), 0)
        hit = rows == edge_list(sizes, lists_ref, m)
        scatter_ref[:, m * part : (m + 1) * part] = jnp.where(hit, 1.0, 0.0).astype(BF)
    nb = basis_t_ref.shape[0]
    pick = lax.broadcasted_iota(jnp.int32, (nb, nb), 0) == slot_ref[...]
    based_t = dot(jnp.where(pick, 1.0, 0.0).astype(BF), basis_t_ref[...])
    based_t_ref[...] = based_t.astype(BF)
    based_ref[...] = based_t.T.astype(BF)


def product_kernel(left_ref, right_ref, out_ref):
    out_ref[...] = dot(left_ref[...], right_ref[...]).astype(BF)


def shared(sizes):
    grps, rows, cols = sizes
    a = lax.axis_index("grp") * rows + lax.axis_index("row")
    c = lax.axis_index("col")

    def partner(at, count, odd):
        up = at % 2 == odd
        return jnp.where(up, at + 1 < count, at > 0)

    return [
        partner(c, cols, 0),
        partner(c, cols, 1),
        partner(a, grps * rows, 0),
        partner(a, grps * rows, 1),
    ]


def scattered(sizes, scatter_ref, near, which):
    part = near[0].shape[0]
    there = shared(sizes)
    total = None
    for m, got in zip(which, near):
        got = jnp.where(there[m], got[...], jnp.zeros_like(got))
        add = dot(scatter_ref[:, m * part : (m + 1) * part], got)
        total = add if total is None else total + add
    return total


def early_kernel(sizes, load_ref, applied_ref, scatter_ref, n0, n2, out_ref):
    out_ref[...] = load_ref[...] - applied_ref[...] - scattered(sizes, scatter_ref, (n0, n2), (0, 2))


def resid_kernel(sizes, early_ref, scatter_ref, based_t_ref, n1, n3, resid_ref, coarse_ref):
    resid = (early_ref[...] - scattered(sizes, scatter_ref, (n1, n3), (1, 3))).astype(BF)
    resid_ref[...] = resid
    coarse_ref[...] = dot(based_t_ref[...], resid).astype(BF)


def pick_kernel(sel_ref, whole_ref, fix_ref, *edges):
    part = edges[0].shape[0]
    for m, edge in enumerate(edges):
        rows = slice(m * part, (m + 1) * part)
        own = dot(sel_ref[rows, :], whole_ref[...])
        fix_ref[rows, :] = own
        edge[...] = own.astype(BF)


def fix_kernel(pre_sel_ref, resid_ref, fix_ref, *edges):
    part = edges[0].shape[0]
    for m, edge in enumerate(edges):
        rows = slice(m * part, (m + 1) * part)
        fix = dot(pre_sel_ref[rows, :], resid_ref[...])
        fix_ref[rows, :] = fix
        edge[...] = fix.astype(BF)


def smoothed(sizes, u, fix_ref, scatter_ref, near, which):
    part = near[0].shape[0]
    there = shared(sizes)
    total = None
    for m, got in zip(which, near):
        rows = slice(m * part, (m + 1) * part)
        fix = fix_ref[rows, :]
        both = jnp.where(there[m], 0.5 * (fix + got[...].astype(F32)), fix).astype(BF)
        add = dot(scatter_ref[:, rows], both)
        total = add if total is None else total + add
    return u + OMEGA * total


def first_kernel(sizes, u_ref, fix_ref, scatter_ref, n0, n2, out_ref):
    out_ref[...] = smoothed(sizes, u_ref[...], fix_ref, scatter_ref, (n0, n2), (0, 2))


def middle_kernel(sizes, op_ref, u_ref, fix_ref, scatter_ref, n1, n3, out_ref, applied_ref):
    u = smoothed(sizes, u_ref[...], fix_ref, scatter_ref, (n1, n3), (1, 3))
    out_ref[...] = u
    applied_ref[...] = dot(op_ref[...], u.astype(BF))


def solution_of(mine_ref, others):
    solved = mine_ref[...]
    for other in others:
        solved = solved + other[...].astype(F32)
    return solved.astype(BF)


def next_kernel(lift_ref, sel_ref, applied_ref, mine_ref, *refs):
    others, (solved_ref, out_ref, *edges) = refs[:-6], refs[-6:]
    solved = solution_of(mine_ref, others)
    solved_ref[...] = solved
    applied = applied_ref[...] + OMEGA * dot(lift_ref[...], solved)
    out_ref[...] = applied
    split_edges(applied, sel_ref, edges)


def late_kernel(sizes, u_ref, fix_ref, scatter_ref, based_ref, solved_ref, n1, n3, out_ref):
    u = u_ref[...] + OMEGA * dot(based_ref[...], solved_ref[...])
    out_ref[...] = smoothed(sizes, u, fix_ref, scatter_ref, (n1, n3), (1, 3))


def last_kernel(u_ref, based_ref, mine_ref, *refs):
    others, (out_hbm, total, sems) = refs[:-3], refs[-3:]
    solved = solution_of(mine_ref, others)
    copies = chunk_copies(total, out_hbm, sems, 0, CHUNKS)
    rows = total.shape[0] // CHUNKS
    for k, copy in enumerate(copies):
        at = slice(k * rows, (k + 1) * rows)
        total[at, :] = u_ref[at, :] + OMEGA * dot(based_ref[at, :], solved)
        copy.start()
    for copy in copies:
        copy.wait()


def regroup_kernel(geometry, nb, inverse_ref, *blocks):
    _, ratio, lines = geometry
    c = lax.axis_index("col")
    owner = c // ratio
    for k, block in enumerate(blocks):
        target = k ^ owner
        parity, pair = target % 2, target // 2
        for line in range(lines):
            rows = pl.ds(pl.multiple_of((2 * line + parity) * nb, nb), nb)
            cols = pl.ds(pl.multiple_of(pair * 2 * nb, 2 * nb), 2 * nb)
            block[line * nb : (line + 1) * nb, :] = inverse_ref[rows, cols]


def upper_kernel(top, mine_ref, got_ref, keep_ref, give_ref):
    c = lax.axis_index("col")
    same = c % 2 == c // top
    keep_ref[...] = jnp.where(same, mine_ref[...], got_ref[...])
    give_ref[...] = jnp.where(same, got_ref[...], mine_ref[...])


def lower_kernel(first_ref, second_ref, keep_ref, give_ref):
    low = (lax.axis_index("col") // 2) % 2
    half = first_ref.shape[1] // 2
    for k, source in enumerate((first_ref, second_ref)):
        left, right = source[:, :half], source[:, half:]
        keep_ref[:, k * half : (k + 1) * half] = jnp.where(low == 0, left, right)
        give_ref[:, k * half : (k + 1) * half] = jnp.where(low == 0, right, left)


def pair_kernel(mine_ref, *refs):
    others, out_ref = refs[:-1], refs[-1]
    nb = mine_ref.shape[0]
    g = lax.axis_index("grp")
    for dg, ref in enumerate((mine_ref, *others)):
        out_ref[pl.ds(pl.multiple_of((g ^ dg) * nb, nb), nb), :] = ref[...]


def coarse_kernel(stepwise, geometry, row_size, nb, moves, *refs):
    grid_rows, _, lines = geometry
    width = 2 * nb
    count = 2 if stepwise else grid_rows
    arrays, refs = refs[:count], refs[count:]
    vectors, refs = refs[: len(moves)], refs[len(moves) :]
    mine_ref, others, (stack, total) = refs[0], refs[1:lines], refs[lines:]
    r, c = lax.axis_index("row"), lax.axis_index("col")
    line = c // 2
    for (dr, dc), vector in zip(moves, vectors):
        for core in range(vector.shape[0] // nb):
            at = ((core * row_size + (r ^ dr)) * 2 + ((c % 2) ^ dc)) * nb
            stack[pl.ds(pl.multiple_of(at, nb), nb), :] = vector[core * nb : (core + 1) * nb, :]
    if stepwise:
        blocks = [
            (arrays[k // 2][:, (k % 2) * width : (k % 2 + 1) * width], line ^ (2 * (k % 2) + k // 2)) for k in range(4)
        ]
    else:
        blocks = [(array[...], k ^ (c % grid_rows)) for k, array in enumerate(arrays)]
    acc = None
    for block, owner in blocks:
        part = dot(block, stack[pl.ds(pl.multiple_of(owner * width, width), width), :])
        acc = part if acc is None else acc + part
    total[...] = acc
    for k in range(lines):
        got = total[pl.ds(pl.multiple_of((line ^ k) * nb, nb), nb), :]
        if k == 0:
            mine_ref[...] = got
        else:
            others[k - 1][...] = got.astype(BF)


def in_steps(sizes):
    grps, row_size, cols = sizes
    return grps * row_size == 4 and cols == 2 * grps * row_size


def body(load, guess, interface_op, precond, basis, coarse_inverse, edge_rows, coarse_slot):
    sizes = tuple(lax.axis_size(axis) for axis in AXES)
    grps, row_size, cols = sizes
    grid_rows = grps * row_size
    load, u, op, pre = load[0, 0], guess[0, 0], interface_op[0, 0], precond[0, 0]
    basis_t = jnp.swapaxes(basis[0, 0], 0, 1)
    slot, lists = coarse_slot[0], edge_rows[0]
    n, cases = load.shape
    nb = basis_t.shape[0]
    part = n // 4
    ratio, lines = cols // grid_rows, cols // 2
    geometry = (grid_rows, ratio, lines)

    halo_pairs = [matching(sizes, m % 2, m < 2) for m in range(4)]
    far_moves = [(dr, dc) for dr in range(row_size) for dc in range(2)]

    def swap_pairs(dg, dr, dc):
        return pairs_of(sizes, lambda g, r, c: (g ^ dg, r ^ dr, c ^ dc))

    def target(k):
        return pairs_of(sizes, lambda g, r, c: (g, r, (c % ratio) * grid_rows + (k ^ (c // ratio))))

    field = shape((n, cases), F32)
    edge = shape((part, cases), BF)
    square = shape((n, n), BF)
    thin = shape((n, nb), BF)
    vector = shape((nb, cases), BF)
    flops = 2 * n * n * cases

    def halo(edges):
        return [send(e, p) for e, p in zip(edges, halo_pairs)]

    stepwise = in_steps(sizes)
    half = shape((lines * nb, coarse_inverse.shape[1]), BF)
    lists, sel, op, u, *halves = call(
        functools.partial(load_kernel, sizes, nb),
        [shape(lists.shape, lists.dtype), square, square, field] + [half, half] * stepwise,
        [lists, op, u] + [coarse_inverse] * stepwise,
        n * n,
        [pltpu.SemaphoreType.DMA((1 + 2 * CHUNKS + 2 * lines,))],
        far=(0, 1, 2, 3),
    )
    if stepwise:
        keep, give = halves
        got = send(give, swap_pairs(0, 0, 1))
    else:
        blocks = call(
            functools.partial(regroup_kernel, geometry, nb),
            [shape((lines * nb, 2 * nb), BF)] * grid_rows,
            [coarse_inverse],
            n,
        )
        blocks = [send(block, target(k)) for k, block in enumerate(blocks)]
    applied, *edges = call(apply_kernel, [field] + [edge] * 4, [op, u, sel], 2 * flops)
    near = halo(edges)
    if stepwise:
        keep, give = call(functools.partial(upper_kernel, cols // 2), [half, half], [keep, got], n)
        got = send(give, swap_pairs(0, 0, cols // 2))
    scatter, based, based_t = call(
        functools.partial(tables_kernel, sizes), [square, thin, shape((nb, n), BF)], [lists, basis_t, slot], n * n
    )
    if stepwise:
        keep, give = call(lower_kernel, [half, half], [keep, got], n)
        blocks = [keep, send(give, swap_pairs(0, 0, 2))]
    for sweep in range(ITERS):
        if sweep == 1:
            pre_sel = call(product_kernel, square, [sel, pre], 2 * n * n * n)
        early = call(
            functools.partial(early_kernel, sizes), field, [load, applied, scatter, near[0], near[2]], flops // 2
        )
        resid, coarse = call(
            functools.partial(resid_kernel, sizes),
            [shape((n, cases), BF), vector],
            [early, scatter, based_t, near[1], near[3]],
            flops // 2,
        )
        cores = [coarse] + [send(coarse, swap_pairs(dg, 0, 0)) for dg in range(1, grps)]
        pair = call(pair_kernel, shape((grps * nb, cases), BF), cores, n)
        vectors = [send(pair, swap_pairs(0, dr, dc)) if dr + dc else pair for dr, dc in far_moves]
        if sweep:
            fix, *own = call(fix_kernel, [field] + [edge] * 4, [pre_sel, resid], flops)
        else:
            whole = call(product_kernel, shape((n, cases), BF), [pre, resid], flops)
            fix, *own = call(pick_kernel, [field] + [edge] * 4, [sel, whole], flops)
        near = halo(own)
        mine, *others = call(
            functools.partial(coarse_kernel, stepwise, geometry, row_size, nb, far_moves),
            [shape((nb, cases), F32)] + [vector] * (lines - 1),
            [*blocks, *vectors],
            2 * lines * nb * 2 * nb * grid_rows * cases,
            [pltpu.VMEM((2 * grid_rows * nb, cases), BF), pltpu.VMEM((lines * nb, cases), F32)],
        )
        others = [send(o, swap_pairs(0, 0, 2 * (k + 1))) for k, o in enumerate(others)]
        u = call(functools.partial(first_kernel, sizes), field, [u, fix, scatter, near[0], near[2]], flops // 2)
        if sweep < ITERS - 1:
            if sweep == 0:
                lift = call(product_kernel, thin, [op, based], n * n * nb)
            u, applied = call(
                functools.partial(middle_kernel, sizes), [field] * 2, [op, u, fix, scatter, near[1], near[3]], 2 * flops
            )
            solved, applied, *edges = call(
                next_kernel, [vector, field] + [edge] * 4, [lift, sel, applied, mine, *others], flops
            )
            near = halo(edges)
        else:
            u = call(
                functools.partial(late_kernel, sizes),
                field,
                [u, fix, scatter, based, solved, near[1], near[3]],
                flops // 2,
            )
            u = call(
                last_kernel,
                field,
                [u, based, mine, *others],
                n * nb * cases,
                [pltpu.VMEM((n, cases), F32), pltpu.SemaphoreType.DMA((CHUNKS,))],
                far_out=True,
            )
    return u[None, None]


def solution(mesh):
    cells = P(("grp", "row"), "col", None, None)
    lists = P(("grp", "row"), "col", None)

    return jax.shard_map(
        body,
        mesh=mesh,
        in_specs=(cells, cells, cells, cells, cells, P(("grp", "row"), "col"), lists, lists),
        out_specs=cells,
        check_vma=False,
    )
```

```python
import functools

import jax
import jax.numpy as jnp
from jax import lax
from jax.experimental import pallas as pl
from jax.experimental.pallas import tpu as pltpu
from jax.sharding import PartitionSpec as P


ITERS = 2
OMEGA = 0.6
AXES = ("grp", "row", "col")
BF = jnp.bfloat16
F32 = jnp.float32
VMEM_LIMIT = 24 << 20
CHUNKS = 4


def dot(a, b):
    return jnp.dot(a, b, preferred_element_type=F32)


def call(kernel, outs, args, flops, scratch=(), far=(), far_out=False):
    moved = sum(a.size * a.dtype.itemsize for a in args)
    vmem, hbm = pl.BlockSpec(memory_space=pltpu.VMEM), pl.BlockSpec(memory_space=pltpu.HBM)
    out_spec = hbm if far_out else vmem
    args = [pltpu.with_memory_space_constraint(a, pltpu.HBM) if k in far else a for k, a in enumerate(args)]
    return pl.pallas_call(
        kernel,
        out_shape=outs,
        in_specs=[hbm if k in far else vmem for k in range(len(args))],
        out_specs=[out_spec] * len(outs) if isinstance(outs, list) else out_spec,
        scratch_shapes=list(scratch),
        compiler_params=pltpu.CompilerParams(vmem_limit_bytes=VMEM_LIMIT),
        cost_estimate=pl.CostEstimate(flops=flops, transcendentals=0, bytes_accessed=moved),
    )(*args)


def chunk_copies(source, target, sems, first, count):
    rows = source.shape[0] // count
    return [
        pltpu.make_async_copy(
            source.at[pl.ds(k * rows, rows)], target.at[pl.ds(k * rows, rows)], sems.at[first + k]
        )
        for k in range(count)
    ]


def shape(dims, dtype):
    return jax.ShapeDtypeStruct(tuple(dims), dtype)


def pairs_of(sizes, where):
    grps, rows, cols = sizes
    flat = lambda g, r, c: (g * rows + r) * cols + c
    return [
        (flat(g, r, c), flat(*where(g, r, c)))
        for g in range(grps)
        for r in range(rows)
        for c in range(cols)
    ]


def matching(sizes, odd, along_cols):
    grps, rows, cols = sizes
    count = cols if along_cols else grps * rows

    def where(g, r, c):
        at = c if along_cols else g * rows + r
        to = at + 1 if at % 2 == odd else at - 1
        if 0 <= to < count:
            return (g, r, to) if along_cols else (to // rows, to % rows, c)
        if along_cols and grps == 2:
            return (1 - g, r, c)
        if not along_cols:
            to = count - 1 - at
            return (to // rows, to % rows, c)
        return (g, r, c)

    return pairs_of(sizes, where)


def send(value, pairs):
    return lax.ppermute(value, AXES, pairs)


def edge_of(sizes, m):
    _, rows, _ = sizes
    if m < 2:
        at, up, down = lax.axis_index("col"), 1, 0
    else:
        at, up, down = lax.axis_index("grp") * rows + lax.axis_index("row"), 3, 2
    return jnp.where(at % 2 == m % 2, up, down)


def edge_list(sizes, lists_ref, m):
    part = lists_ref.shape[1] // 4
    at = pl.multiple_of(edge_of(sizes, m) * part, part)
    return lists_ref[:, pl.ds(at, part)]


def load_kernel(sizes, nb, lists_hbm, op_hbm, u_hbm, *refs):
    if len(refs) > 5:
        inverse_hbm, lists_ref, sel_ref, op_ref, u_ref, keep_ref, give_ref, sems = refs
    else:
        lists_ref, sel_ref, op_ref, u_ref, sems = refs
    named = pltpu.make_async_copy(lists_hbm, lists_ref, sems.at[0])
    copies = []
    if len(refs) > 5:
        parity = lax.axis_index("col") % 2
        lines = keep_ref.shape[0] // nb
        for line in range(lines):
            for k, (ref, mine) in enumerate(((keep_ref, parity), (give_ref, 1 - parity))):
                rows = pl.ds(pl.multiple_of((2 * line + mine) * nb, nb), nb)
                sem = sems.at[1 + 2 * CHUNKS + 2 * line + k]
                copies.append(pltpu.make_async_copy(inverse_hbm.at[rows], ref.at[pl.ds(line * nb, nb)], sem))
    copies += chunk_copies(u_hbm, u_ref, sems, 1, CHUNKS)
    copies += chunk_copies(op_hbm, op_ref, sems, 1 + CHUNKS, CHUNKS)
    for copy in [named] + copies:
        copy.start()
    named.wait()
    n = sel_ref.shape[0]
    part = n // 4
    for m in range(4):
        names = jnp.broadcast_to(edge_list(sizes, lists_ref, m), (128, part)).T
        lanes = lax.broadcasted_iota(jnp.int32, (part, 128), 1)
        for j in range(n // 128):
            hit = names == lanes + j * 128
            sel_ref[m * part : (m + 1) * part, j * 128 : (j + 1) * 128] = jnp.where(hit, 1.0, 0.0).astype(BF)
    for copy in copies:
        copy.wait()


def apply_kernel(op_ref, u_ref, sel_ref, applied_ref, *edges):
    applied = dot(op_ref[...], u_ref[...].astype(BF))
    applied_ref[...] = applied
    split_edges(applied, sel_ref, edges)


def split_edges(field, sel_ref, edges):
    field = field.astype(BF)
    part = edges[0].shape[0]
    for m, edge in enumerate(edges):
        edge[...] = dot(sel_ref[m * part : (m + 1) * part, :], field).astype(BF)


def tables_kernel(sizes, lists_ref, basis_t_ref, slot_ref, scatter_ref, based_ref, based_t_ref, listed_ref):
    n = scatter_ref.shape[0]
    part = n // 4
    for m in range(4):
        rows = lax.broadcasted_iota(jnp.int32, (n, part), 0)
        hit = rows == edge_list(sizes, lists_ref, m)
        scatter_ref[:, m * part : (m + 1) * part] = jnp.where(hit, 1.0, 0.0).astype(BF)
    nb = basis_t_ref.shape[0]
    pick = lax.broadcasted_iota(jnp.int32, (nb, nb), 0) == slot_ref[...]
    based_t = dot(jnp.where(pick, 1.0, 0.0).astype(BF), basis_t_ref[...])
    based_t_ref[...] = based_t.astype(BF)
    based_ref[...] = based_t.T.astype(BF)
    listed_ref[...] = dot(based_t.astype(BF), scatter_ref[...]).astype(BF)


def product_kernel(left_ref, right_ref, out_ref):
    out_ref[...] = dot(left_ref[...], right_ref[...]).astype(BF)


def shared(sizes):
    grps, rows, cols = sizes
    a = lax.axis_index("grp") * rows + lax.axis_index("row")
    c = lax.axis_index("col")

    def partner(at, count, odd):
        up = at % 2 == odd
        return jnp.where(up, at + 1 < count, at > 0)

    return [
        partner(c, cols, 0),
        partner(c, cols, 1),
        partner(a, grps * rows, 0),
        partner(a, grps * rows, 1),
    ]


def scattered(sizes, scatter_ref, near, which):
    part = near[0].shape[0]
    there = shared(sizes)
    total = None
    for m, got in zip(which, near):
        got = jnp.where(there[m], got[...], jnp.zeros_like(got))
        add = dot(scatter_ref[:, m * part : (m + 1) * part], got)
        total = add if total is None else total + add
    return total


def early_kernel(sizes, load_ref, applied_ref, scatter_ref, based_t_ref, n0, n2, out_ref, coarse_ref):
    early = load_ref[...] - applied_ref[...] - scattered(sizes, scatter_ref, (n0, n2), (0, 2))
    out_ref[...] = early
    coarse_ref[...] = dot(based_t_ref[...], early.astype(BF))


def vector_kernel(sizes, early_ref, lists_ref, n1, n3, coarse_ref):
    part = n1.shape[0]
    there = shared(sizes)
    total = early_ref[...]
    for m, got in ((1, n1), (3, n3)):
        got = jnp.where(there[m], got[...], jnp.zeros_like(got))
        total = total - dot(lists_ref[:, m * part : (m + 1) * part], got)
    coarse_ref[...] = total.astype(BF)


def resid_kernel(sizes, early_ref, scatter_ref, n1, n3, resid_ref):
    resid_ref[...] = (early_ref[...] - scattered(sizes, scatter_ref, (n1, n3), (1, 3))).astype(BF)


def pick_kernel(sel_ref, whole_ref, fix_ref, *edges):
    part = edges[0].shape[0]
    for m, edge in enumerate(edges):
        rows = slice(m * part, (m + 1) * part)
        own = dot(sel_ref[rows, :], whole_ref[...])
        fix_ref[rows, :] = own
        edge[...] = own.astype(BF)


def fix_kernel(pre_sel_ref, resid_ref, fix_ref, *edges):
    part = edges[0].shape[0]
    for m, edge in enumerate(edges):
        rows = slice(m * part, (m + 1) * part)
        fix = dot(pre_sel_ref[rows, :], resid_ref[...])
        fix_ref[rows, :] = fix
        edge[...] = fix.astype(BF)


def smoothed(sizes, u, fix_ref, scatter_ref, near, which):
    part = near[0].shape[0]
    there = shared(sizes)
    total = None
    for m, got in zip(which, near):
        rows = slice(m * part, (m + 1) * part)
        fix = fix_ref[rows, :]
        both = jnp.where(there[m], 0.5 * (fix + got[...].astype(F32)), fix).astype(BF)
        add = dot(scatter_ref[:, rows], both)
        total = add if total is None else total + add
    return u + OMEGA * total


def first_kernel(sizes, u_ref, fix_ref, scatter_ref, n0, n2, out_ref):
    out_ref[...] = smoothed(sizes, u_ref[...], fix_ref, scatter_ref, (n0, n2), (0, 2))


def middle_kernel(sizes, op_ref, u_ref, fix_ref, scatter_ref, n1, n3, out_ref, applied_ref):
    u = smoothed(sizes, u_ref[...], fix_ref, scatter_ref, (n1, n3), (1, 3))
    out_ref[...] = u
    applied_ref[...] = dot(op_ref[...], u.astype(BF))


def solution_of(mine_ref, others):
    solved = mine_ref[...]
    for other in others:
        solved = solved + other[...].astype(F32)
    return solved.astype(BF)


def next_kernel(lift_ref, sel_ref, applied_ref, mine_ref, *refs):
    others, (solved_ref, out_ref, *edges) = refs[:-6], refs[-6:]
    solved = solution_of(mine_ref, others)
    solved_ref[...] = solved
    applied = applied_ref[...] + OMEGA * dot(lift_ref[...], solved)
    out_ref[...] = applied
    split_edges(applied, sel_ref, edges)


def late_kernel(sizes, u_ref, fix_ref, scatter_ref, based_ref, solved_ref, n1, n3, out_ref):
    u = u_ref[...] + OMEGA * dot(based_ref[...], solved_ref[...])
    out_ref[...] = smoothed(sizes, u, fix_ref, scatter_ref, (n1, n3), (1, 3))


def last_kernel(u_ref, based_ref, mine_ref, *refs):
    others, (out_hbm, total, sems) = refs[:-3], refs[-3:]
    solved = solution_of(mine_ref, others)
    copies = chunk_copies(total, out_hbm, sems, 0, CHUNKS)
    rows = total.shape[0] // CHUNKS
    for k, copy in enumerate(copies):
        at = slice(k * rows, (k + 1) * rows)
        total[at, :] = u_ref[at, :] + OMEGA * dot(based_ref[at, :], solved)
        copy.start()
    for copy in copies:
        copy.wait()


def regroup_kernel(geometry, nb, inverse_ref, *blocks):
    _, ratio, lines = geometry
    c = lax.axis_index("col")
    owner = c // ratio
    for k, block in enumerate(blocks):
        target = k ^ owner
        parity, pair = target % 2, target // 2
        for line in range(lines):
            rows = pl.ds(pl.multiple_of((2 * line + parity) * nb, nb), nb)
            cols = pl.ds(pl.multiple_of(pair * 2 * nb, 2 * nb), 2 * nb)
            block[line * nb : (line + 1) * nb, :] = inverse_ref[rows, cols]


def upper_kernel(top, mine_ref, got_ref, keep_ref, give_ref):
    c = lax.axis_index("col")
    same = c % 2 == c // top
    keep_ref[...] = jnp.where(same, mine_ref[...], got_ref[...])
    give_ref[...] = jnp.where(same, got_ref[...], mine_ref[...])


def lower_kernel(first_ref, second_ref, keep_ref, give_ref):
    low = (lax.axis_index("col") // 2) % 2
    half = first_ref.shape[1] // 2
    for k, source in enumerate((first_ref, second_ref)):
        left, right = source[:, :half], source[:, half:]
        keep_ref[:, k * half : (k + 1) * half] = jnp.where(low == 0, left, right)
        give_ref[:, k * half : (k + 1) * half] = jnp.where(low == 0, right, left)


def pair_kernel(mine_ref, *refs):
    others, out_ref = refs[:-1], refs[-1]
    nb = mine_ref.shape[0]
    g = lax.axis_index("grp")
    for dg, ref in enumerate((mine_ref, *others)):
        out_ref[pl.ds(pl.multiple_of((g ^ dg) * nb, nb), nb), :] = ref[...]


def coarse_kernel(stepwise, geometry, row_size, nb, moves, *refs):
    grid_rows, _, lines = geometry
    width = 2 * nb
    count = 2 if stepwise else grid_rows
    arrays, refs = refs[:count], refs[count:]
    vectors, refs = refs[: len(moves)], refs[len(moves) :]
    mine_ref, others, (stack, total) = refs[0], refs[1:lines], refs[lines:]
    r, c = lax.axis_index("row"), lax.axis_index("col")
    line = c // 2
    for (dr, dc), vector in zip(moves, vectors):
        for core in range(vector.shape[0] // nb):
            at = ((core * row_size + (r ^ dr)) * 2 + ((c % 2) ^ dc)) * nb
            stack[pl.ds(pl.multiple_of(at, nb), nb), :] = vector[core * nb : (core + 1) * nb, :]
    if stepwise:
        blocks = [
            (arrays[k // 2][:, (k % 2) * width : (k % 2 + 1) * width], line ^ (2 * (k % 2) + k // 2)) for k in range(4)
        ]
    else:
        blocks = [(array[...], k ^ (c % grid_rows)) for k, array in enumerate(arrays)]
    acc = None
    for block, owner in blocks:
        part = dot(block, stack[pl.ds(pl.multiple_of(owner * width, width), width), :])
        acc = part if acc is None else acc + part
    total[...] = acc
    for k in range(lines):
        got = total[pl.ds(pl.multiple_of((line ^ k) * nb, nb), nb), :]
        if k == 0:
            mine_ref[...] = got
        else:
            others[k - 1][...] = got.astype(BF)


def in_steps(sizes):
    grps, row_size, cols = sizes
    return grps * row_size == 4 and cols == 2 * grps * row_size


def body(load, guess, interface_op, precond, basis, coarse_inverse, edge_rows, coarse_slot):
    sizes = tuple(lax.axis_size(axis) for axis in AXES)
    grps, row_size, cols = sizes
    grid_rows = grps * row_size
    load, u, op, pre = load[0, 0], guess[0, 0], interface_op[0, 0], precond[0, 0]
    basis_t = jnp.swapaxes(basis[0, 0], 0, 1)
    slot, lists = coarse_slot[0], edge_rows[0]
    n, cases = load.shape
    nb = basis_t.shape[0]
    part = n // 4
    ratio, lines = cols // grid_rows, cols // 2
    geometry = (grid_rows, ratio, lines)

    halo_pairs = [matching(sizes, m % 2, m < 2) for m in range(4)]
    far_moves = [(dr, dc) for dr in range(row_size) for dc in range(2)]

    def swap_pairs(dg, dr, dc):
        return pairs_of(sizes, lambda g, r, c: (g ^ dg, r ^ dr, c ^ dc))

    def target(k):
        return pairs_of(sizes, lambda g, r, c: (g, r, (c % ratio) * grid_rows + (k ^ (c // ratio))))

    field = shape((n, cases), F32)
    edge = shape((part, cases), BF)
    square = shape((n, n), BF)
    thin = shape((n, nb), BF)
    vector = shape((nb, cases), BF)
    flops = 2 * n * n * cases

    def halo(edges):
        return [send(e, p) for e, p in zip(edges, halo_pairs)]

    stepwise = in_steps(sizes)
    half = shape((lines * nb, coarse_inverse.shape[1]), BF)
    lists, sel, op, u, *halves = call(
        functools.partial(load_kernel, sizes, nb),
        [shape(lists.shape, lists.dtype), square, square, field] + [half, half] * stepwise,
        [lists, op, u] + [coarse_inverse] * stepwise,
        n * n,
        [pltpu.SemaphoreType.DMA((1 + 2 * CHUNKS + 2 * lines,))],
        far=(0, 1, 2, 3),
    )
    if stepwise:
        keep, give = halves
        got = send(give, swap_pairs(0, 0, 1))
    else:
        blocks = call(
            functools.partial(regroup_kernel, geometry, nb),
            [shape((lines * nb, 2 * nb), BF)] * grid_rows,
            [coarse_inverse],
            n,
        )
        blocks = [send(block, target(k)) for k, block in enumerate(blocks)]
    applied, *edges = call(apply_kernel, [field] + [edge] * 4, [op, u, sel], 2 * flops)
    near = halo(edges)
    if stepwise:
        keep, give = call(functools.partial(upper_kernel, cols // 2), [half, half], [keep, got], n)
        got = send(give, swap_pairs(0, 0, cols // 2))
    scatter, based, based_t, listed = call(
        functools.partial(tables_kernel, sizes),
        [square, thin, shape((nb, n), BF), shape((nb, n), BF)],
        [lists, basis_t, slot],
        n * n,
    )
    if stepwise:
        keep, give = call(lower_kernel, [half, half], [keep, got], n)
        blocks = [keep, send(give, swap_pairs(0, 0, 2))]
    for sweep in range(ITERS):
        if sweep == 1:
            pre_sel = call(product_kernel, square, [sel, pre], 2 * n * n * n)
        early, coarse_part = call(
            functools.partial(early_kernel, sizes),
            [field, shape((nb, cases), F32)],
            [load, applied, scatter, based_t, near[0], near[2]],
            flops // 2,
        )
        coarse = call(
            functools.partial(vector_kernel, sizes), vector, [coarse_part, listed, near[1], near[3]], n * nb * cases
        )
        resid = call(
            functools.partial(resid_kernel, sizes),
            shape((n, cases), BF),
            [early, scatter, near[1], near[3]],
            flops // 2,
        )
        cores = [coarse] + [send(coarse, swap_pairs(dg, 0, 0)) for dg in range(1, grps)]
        pair = call(pair_kernel, shape((grps * nb, cases), BF), cores, n)
        vectors = [send(pair, swap_pairs(0, dr, dc)) if dr + dc else pair for dr, dc in far_moves]
        if sweep:
            fix, *own = call(fix_kernel, [field] + [edge] * 4, [pre_sel, resid], flops)
        else:
            whole = call(product_kernel, shape((n, cases), BF), [pre, resid], flops)
            fix, *own = call(pick_kernel, [field] + [edge] * 4, [sel, whole], flops)
        near = halo(own)
        mine, *others = call(
            functools.partial(coarse_kernel, stepwise, geometry, row_size, nb, far_moves),
            [shape((nb, cases), F32)] + [vector] * (lines - 1),
            [*blocks, *vectors],
            2 * lines * nb * 2 * nb * grid_rows * cases,
            [pltpu.VMEM((2 * grid_rows * nb, cases), BF), pltpu.VMEM((lines * nb, cases), F32)],
        )
        others = [send(o, swap_pairs(0, 0, 2 * (k + 1))) for k, o in enumerate(others)]
        u = call(functools.partial(first_kernel, sizes), field, [u, fix, scatter, near[0], near[2]], flops // 2)
        if sweep < ITERS - 1:
            if sweep == 0:
                lift = call(product_kernel, thin, [op, based], n * n * nb)
            u, applied = call(
                functools.partial(middle_kernel, sizes), [field] * 2, [op, u, fix, scatter, near[1], near[3]], 2 * flops
            )
            solved, applied, *edges = call(
                next_kernel, [vector, field] + [edge] * 4, [lift, sel, applied, mine, *others], flops
            )
            near = halo(edges)
        else:
            u = call(
                functools.partial(late_kernel, sizes),
                field,
                [u, fix, scatter, based, solved, near[1], near[3]],
                flops // 2,
            )
            u = call(
                last_kernel,
                field,
                [u, based, mine, *others],
                n * nb * cases,
                [pltpu.VMEM((n, cases), F32), pltpu.SemaphoreType.DMA((CHUNKS,))],
                far_out=True,
            )
    return u[None, None]


def solution(mesh):
    cells = P(("grp", "row"), "col", None, None)
    lists = P(("grp", "row"), "col", None)

    return jax.shard_map(
        body,
        mesh=mesh,
        in_specs=(cells, cells, cells, cells, cells, P(("grp", "row"), "col"), lists, lists),
        out_specs=cells,
        check_vma=False,
    )
```
